128 devices in a mesh: expert: 32 (over z, y, core), helper: 4 (over x).
Axes of the slice: x: 4, y: 4, z: 4, core: 2. Of those that a mesh axis runs over, the one named last changes fastest.
Arguments:
- tokens: bfloat16 [131072, 768], P(('expert', 'helper')), may hold values from -6 to 6
- gate: float32 [131072], P(('expert', 'helper')), may hold values from 0.2 to 1
- expert_ids: int32 [131072, 1], P(('expert', 'helper')), may hold values from 0 to 127; in each aligned block of 1024 rows (0 to 1023, 1024 to 2047, ...) at most 12 rows name the same one
- backup_ids: int32 [131072, 1], P(('expert', 'helper')), may hold values from 0 to 127; in each aligned block of 1024 rows (0 to 1023, 1024 to 2047, ...) at most 12 rows name the same one
- capacity: int32 [128], replicated, may hold values from 2 to 12
- w_in: bfloat16 [128, 768, 3072], P('expert', None, 'helper'), may hold values from -0.21875 to 0.21875
- w_out: bfloat16 [128, 3072, 768], P('expert', 'helper'), may hold values from -0.109375 to 0.109375
Outputs:
- mixed: bfloat16 [131072, 768], P(('expert', 'helper'))
The draws below stay inside these ranges and needn't reach their ends.
Inputs may be any that keep to these rules, and one draw needn't show every extreme that they name: `expert_ids`: in the rows of one device no expert is the first expert of more than 12 rows; some expert reaches 12. `backup_ids`: in the rows of one device no expert is the backup of more than 12 rows; some expert reaches 12.
All inputs are finite; a program needn't handle non-finite values.
Results may differ from the reference program's by a relative error of at most 0.0095.
Values may be sent and summed in bfloat16 or wider, within the bound.
No kernel may reach another device: no remote copies, remote signals or barrier semaphores. Data moves between devices by JAX's collectives and lax.ppermute only.
A program may use at most 192 MiB of HBM per device.

```python
import math
import jax
import jax.numpy as jnp
import numpy as np
from jax import lax

D = 768
FF = 3072
TOK_DEV = 1024
EXPERTS = 128
SLOT = 12
TOKENS = 131072
N_EXPERT = 32
N_HELPER = 4


def touch_ends(entries, stream_key, low, largest):
    place = [jax.random.randint(jax.random.fold_in(stream_key, axis), (), 0, length) for axis, length in enumerate(entries.shape)]
    longest = entries.shape.index(max(entries.shape))
    next_to = place[:longest] + [(place[longest] + 1) % entries.shape[longest]] + place[longest + 1:]
    return entries.at[tuple(place)].set(low).at[tuple(next_to)].set(largest)


def level_of(own_key, extent, pieces, smallest, high):
    def one(axis_at, blocks):
        steps = jax.random.uniform(jax.random.fold_in(jax.random.fold_in(own_key, 6), axis_at), (blocks,), jnp.float32, smallest / len(pieces), high / len(pieces))
        return jnp.repeat(jnp.exp(steps), extent[axis_at] // blocks).reshape((-1,) + (1,) * (len(extent) - axis_at - 1))

    loudness = one(*pieces[0])
    for cut in pieces[1:]:
        loudness = loudness * one(*cut)
    return loudness


def shared_out(stream_key, own, number, rows, count, top, reach, skew):
    sequence = jax.random.permutation(stream_key, count)
    crowded, ordinary = shares(count, rows * top, reach, skew, True), shares(count, rows * top, reach, skew, False)
    places = jnp.arange(count)

    def named(tallies, turn):
        used = int((tallies > 0).sum())
        fixed = max(1, used // 4)
        shifted = fixed + (places - fixed + turn * (used - fixed)) % max(1, count - fixed)
        return jnp.zeros((count,), jnp.int32).at[sequence[jnp.where(places < fixed, places, shifted)]].set(jnp.asarray(tallies, jnp.int32))

    tallies = jnp.where(number % 4 == 0, named(crowded, number // 4), named(ordinary, number - number // 4 - 1))
    mixed = jax.random.permutation(jax.random.fold_in(own, 3), count)
    giver, receiver = mixed[0:count // 2 * 2:2], mixed[1:count // 2 * 2:2]
    margin = jnp.minimum(tallies[giver] - 1, reach - tallies[receiver]) // 2
    margin = jnp.where((giver == sequence[0]) | (receiver == sequence[0]) | (tallies[receiver] == 0), 0, jnp.maximum(margin, 0))
    shifted = jax.random.randint(jax.random.fold_in(own, 4), (count // 2,), 0, 1 << 20) % (margin + 1)
    tallies = tallies.at[giver].add(-shifted).at[receiver].add(shifted)
    items = jnp.searchsorted(jnp.cumsum(tallies), jnp.arange(rows * top), side="right").astype(jnp.int32)
    listing = items.reshape(top, rows).T
    listing = listing[jax.random.permutation(jax.random.fold_in(own, 1), rows)]
    turn = jax.random.randint(jax.random.fold_in(own, 2), (rows, 1), 0, top)
    return jnp.take_along_axis(listing, (jnp.arange(top)[None, :] + turn) % top, axis=1)


def shares(amount, total, reach, lean, full):
    portions = [(1 << 20) // math.isqrt(rank ** lean) + 1 for rank in range(1, amount + 1)]
    largest = reach if full else min(reach, max(-(-total // amount), total * portions[0] // sum(portions)))
    least = 1 if total - largest >= amount - 1 else 0
    counts, surplus = [largest] + [least] * (amount - 1), total - largest - least * (amount - 1)
    while surplus > 0:
        free = [i for i in range(1, amount) if counts[i] < largest] or [i for i in range(1, amount) if counts[i] < reach]
        whole, budget = sum([portions[i] for i in free]), surplus
        for i in free:
            extra = min(reach - counts[i], max(1, budget * portions[i] // whole), surplus)
            counts[i] = counts[i] + extra
            surplus = surplus - extra
    return np.array(counts)


def centred(stream_key, shape, scale, most, pieces=(), kind=jnp.bfloat16):
    level = level_of(stream_key, shape, pieces, -0.22, 0.18) if pieces else 1.0
    values = jax.random.normal(stream_key, shape, jnp.float32) * scale * level
    return jnp.minimum(jnp.maximum(values, -most), most).astype(kind)


def setup_inputs(seed: int = 0) -> dict:
    arg_keys = jax.random.split(jax.random.key(seed), 8)
    tokens = centred(arg_keys[0], (TOKENS, D), 1.0, 6.0, ((0, 128),))
    gate = jnp.clip(0.2 + 0.8 * jax.random.uniform(arg_keys[1], (TOKENS,), jnp.float32) ** level_of(arg_keys[1], (TOKENS,), ((0, 128),), -0.2, 0.2), 0.2, 1.0)
    expert_ids_keys = jax.random.split(jax.random.fold_in(arg_keys[2], 1), TOKENS // TOK_DEV)
    expert_ids_turns = jax.random.permutation(jax.random.fold_in(arg_keys[2], 3), TOKENS // TOK_DEV)
    expert_ids = jax.vmap(lambda own, number: shared_out(jax.random.fold_in(arg_keys[2], 2), own, number, TOK_DEV, EXPERTS, 1, SLOT, 2))(expert_ids_keys, expert_ids_turns).reshape((TOKENS, 1))
    backup_ids_keys = jax.random.split(jax.random.fold_in(arg_keys[3], 1), TOKENS // TOK_DEV)
    backup_ids_turns = jax.random.permutation(jax.random.fold_in(arg_keys[3], 3), TOKENS // TOK_DEV)
    backup_ids = jax.vmap(lambda own, number: shared_out(jax.random.fold_in(arg_keys[3], 2), own, number, TOK_DEV, EXPERTS, 1, SLOT, 1))(backup_ids_keys, backup_ids_turns).reshape((TOKENS, 1))
    capacity = touch_ends(jax.random.randint(arg_keys[4], (EXPERTS,), 2, SLOT + 1), jax.random.fold_in(arg_keys[4], 1), 2, SLOT).astype(jnp.int32)
    w_in = centred(arg_keys[5], (EXPERTS, D, FF), D ** -0.5, 0.21875, ((0, 32), (2, 4)))
    w_out = centred(arg_keys[6], (EXPERTS, FF, D), FF ** -0.5, 0.109375, ((0, 32), (1, 4)))
    return dict(tokens=tokens, gate=gate, expert_ids=expert_ids, backup_ids=backup_ids, capacity=capacity, w_in=w_in, w_out=w_out)


def assign(first, backup, capacity, count, slot):
    columns = jnp.arange(count, dtype=jnp.int32)
    onehot = (first[:, None] == columns[None, :]).astype(jnp.int32)
    rank = jnp.sum((jnp.cumsum(onehot, axis=0) - onehot) * onehot, axis=1)
    limit = jnp.sum(onehot * capacity[None, :], axis=1)
    kept = rank < limit
    spill = (backup[:, None] == columns[None, :]).astype(jnp.int32) * (1 - kept.astype(jnp.int32))[:, None]
    spill_rank = jnp.sum((jnp.cumsum(spill, axis=0) - spill) * spill, axis=1)
    final = jnp.where(kept, first, backup).astype(jnp.int32)
    slots = jnp.where(kept, rank, slot + spill_rank).astype(jnp.int32)
    return slots, final


def expert_apply(rows, weight_in, weight_out):
    width = weight_in.shape[1] // N_HELPER
    total = jnp.zeros((rows.shape[0], rows.shape[1]), jnp.float32)
    for quarter in range(N_HELPER):
        inner = weight_in[:, quarter * width:(quarter + 1) * width].astype(jnp.float32)
        outer = weight_out[quarter * width:(quarter + 1) * width, :].astype(jnp.float32)
        hidden = jax.nn.relu(jnp.dot(rows.astype(jnp.float32), inner)).astype(jnp.bfloat16)
        part = jnp.dot(hidden.astype(jnp.float32), outer).astype(jnp.bfloat16)
        total = total + part.astype(jnp.float32)
    return total.astype(jnp.bfloat16)


def reference(tokens, gate, expert_ids, backup_ids, capacity, w_in, w_out):
    devices = N_EXPERT * N_HELPER
    room = 2 * SLOT
    first = expert_ids[:, 0].reshape(devices, TOK_DEV)
    backup = backup_ids[:, 0].reshape(devices, TOK_DEV)
    slots, final = jax.vmap(lambda a, b: assign(a, b, capacity, EXPERTS, SLOT))(first, backup)
    owner = jnp.arange(devices, dtype=jnp.int32)[:, None] * room + slots
    owner = owner.reshape(-1)
    final = final.reshape(-1)
    buffer = jnp.zeros((EXPERTS, devices * room, D), jnp.bfloat16).at[final, owner].set(tokens)
    results = lax.map(lambda item: expert_apply(item[0], item[1], item[2]), (buffer, w_in, w_out))
    picked = results[final, owner]
    return (gate[:, None] * picked.astype(jnp.float32)).astype(jnp.bfloat16)
```

```python
import functools

import jax
import jax.numpy as jnp
from jax import lax
from jax.experimental import pallas as pl
from jax.experimental.pallas import tpu as pltpu
from jax.sharding import Mesh
from jax.sharding import PartitionSpec as P

EXPERT = ("expert_0", "expert_1", "expert_2")
EXPERT_HELPER = ("expert_0", "expert_1", "expert_2", "helper")
BIN = 64
ROOM = 512
PAIR_A = [(0, 1), (1, 0), (2, 3), (3, 2)]
PAIR_B = [(1, 2), (2, 1), (3, 0), (0, 3)]
F32 = jnp.float32
BF16 = jnp.bfloat16
VMEM_LIMIT = 24 * 1024 * 1024


def dot(a, b):
    return jnp.dot(a, b, preferred_element_type=F32)


def dot_nt(a, b):
    return lax.dot_general(a, b, (((1,), (1,)), ((), ())), preferred_element_type=F32)


def iota(shape, dim):
    return lax.broadcasted_iota(jnp.int32, shape, dim)


def ones_where(cond):
    return jnp.where(cond, 1.0, 0.0).astype(BF16)


def params():
    return pltpu.CompilerParams(vmem_limit_bytes=VMEM_LIMIT)


def cost(flops, read):
    return pl.CostEstimate(flops=flops, bytes_accessed=read, transcendentals=0)


def route_kernel(held, first_ref, backup_ref, cap_ref, gate_ref, row_ref, col_ref, count_ref):
    count = cap_ref.shape[1]
    toks = first_ref.shape[1]
    lanes = iota((count, toks), 0)
    first = first_ref[...]
    backup = backup_ref[...]
    one = jnp.where(lanes == first, 1.0, 0.0)
    two = jnp.where(lanes == backup, 1.0, 0.0)
    earlier = ones_where(iota((toks, toks), 0) < iota((toks, toks), 1))
    rank = jnp.sum(dot(one.astype(BF16), earlier) * one, axis=0, keepdims=True)
    cap = jnp.broadcast_to(cap_ref[...].astype(F32), (8, count)).astype(BF16)
    limit = dot(cap, one.astype(BF16))[0:1]
    kept = jnp.where(rank < limit, 1.0, 0.0)
    spill = two * (1.0 - kept)
    spill_rank = jnp.sum(dot(spill.astype(BF16), earlier) * spill, axis=0, keepdims=True)
    mine = one * kept
    n_kept = jnp.sum(mine, axis=1, keepdims=True)
    final = mine + spill
    n_all = jnp.sum(final, axis=1, keepdims=True)
    e0, e1 = iota((count, count), 0), iota((count, count), 1)
    before = ones_where((e1 < e0) & (e1 // held == e0 // held))
    start = dot(before, jnp.broadcast_to(n_all, (count, count)).astype(BF16))[:, 0:1]
    place = jnp.sum(final * start + spill * n_kept, axis=0, keepdims=True)
    place = place + jnp.where(kept > 0.5, rank, spill_rank)
    owner = jnp.where(kept > 0.5, first, backup) // held
    row = jnp.where(place < BIN, owner.astype(F32) * BIN + place, -1.0)
    row_ref[...] = jnp.broadcast_to(row, (8, toks)).astype(jnp.int32)
    stacked = jnp.where(
        iota((128, toks), 0) == 0,
        jnp.broadcast_to(row, (128, toks)),
        jnp.broadcast_to(gate_ref[...], (128, toks)),
    )
    col_ref[...] = stacked.T
    every = jnp.ones((8, toks), BF16)
    count_ref[...] = dot_nt(every, final.astype(BF16))[0:1].astype(jnp.int32)


def route(first, backup, capacity, gate, held):
    toks, count = first.shape[1], capacity.shape[1]
    return pl.pallas_call(
        functools.partial(route_kernel, held),
        out_shape=(
            jax.ShapeDtypeStruct((8, toks), jnp.int32),
            jax.ShapeDtypeStruct((toks, 128), F32),
            jax.ShapeDtypeStruct((1, count), jnp.int32),
        ),
        compiler_params=params(),
        cost_estimate=cost(4 * toks * toks * count, toks * 512),
        name="route",
    )(first, backup, capacity, gate)


def pick_kernel(first, index_ref, rows_ref, out_ref):
    count, many = out_ref.shape[0], rows_ref.shape[0]
    here = iota((count, many), 0) + (first + pl.program_id(0) * count)
    out_ref[...] = dot(ones_where(here == index_ref[0:1, :]), rows_ref[...]).astype(BF16)


def pick(index, rows, first, count, blocks, name):
    many, wide = rows.shape
    block = count // blocks
    return pl.pallas_call(
        functools.partial(pick_kernel, first),
        out_shape=jax.ShapeDtypeStruct((count, wide), BF16),
        grid=(blocks,),
        in_specs=[
            pl.BlockSpec((8, many), lambda i: (0, 0)),
            pl.BlockSpec((many, wide), lambda i: (0, 0)),
        ],
        out_specs=pl.BlockSpec((block, wide), lambda i: (i, 0)),
        compiler_params=params(),
        cost_estimate=cost(2 * count * many * wide, 2 * (count + many) * wide),
        name=name,
    )(index, rows)


def places_kernel(held, group_ref, counts_ref, row_ref, col_ref, over_ref):
    sources, count = counts_ref.shape
    total = sources * BIN
    counts = counts_ref[...].astype(F32).astype(BF16)
    fullest = jnp.max(dot(counts, ones_where(iota((count, count), 0) // held == iota((count, count), 1))))
    busiest = jnp.max(dot(jnp.ones((8, sources), BF16), counts))
    over = jnp.where((fullest > BIN) | (busiest > ROOM), 1, 0)
    over_ref[...] = jnp.broadcast_to(over, (8, 128))
    which = iota((8, count), 0)
    mine = ones_where((iota((8, count), 1) == group_ref[0] * held + which) & (which < held))
    n = dot_nt(mine, counts)
    base = dot(n.astype(BF16), ones_where(iota((sources, sources), 0) < iota((sources, sources), 1)))
    begin = jnp.zeros((8, sources), F32)
    for j in range(held):
        ahead = iota((8, sources), 0) > j
        begin = begin + jnp.where(ahead, jnp.broadcast_to(n[j : j + 1], (8, sources)), 0.0)
    shift = base - begin + 128.0
    high = jnp.floor(shift * (1.0 / 128.0))
    low = shift - high * 128.0
    spread = ones_where(iota((sources, total), 1) // BIN == iota((sources, total), 0))
    place = dot(high.astype(BF16), spread) * 128.0 + dot(low.astype(BF16), spread) - 128.0
    begin = dot(begin.astype(BF16), spread)
    end = begin + dot(n.astype(BF16), spread)
    r = (iota((8, total), 1) % BIN).astype(F32)
    place = place + r
    inside = (r >= begin) & (r < end) & (place < ROOM)
    index = jnp.where(inside, place + iota((8, total), 0).astype(F32) * ROOM + 1.0, 0.0)
    index = jnp.sum(index, axis=0, keepdims=True) - 1.0
    row_ref[...] = jnp.broadcast_to(index, (8, total)).astype(jnp.int32)
    col_ref[...] = jnp.broadcast_to(index, (128, total)).T


def places(group, counts, held):
    total = counts.shape[0] * BIN
    return pl.pallas_call(
        functools.partial(places_kernel, held),
        out_shape=(
            jax.ShapeDtypeStruct((8, total), jnp.int32),
            jax.ShapeDtypeStruct((total, 128), F32),
            jax.ShapeDtypeStruct((8, 128), jnp.int32),
        ),
        in_specs=[
            pl.BlockSpec(memory_space=pltpu.SMEM),
            pl.BlockSpec(memory_space=pltpu.VMEM),
        ],
        compiler_params=params(),
        cost_estimate=cost(1 << 27, 1 << 20),
        name="places",
    )(group, counts)


def expert_kernel(steps, rows_ref, in0_ref, out0_ref, in1_ref, out1_ref, part_ref, total_ref):
    k = pl.program_id(0)

    def term(in_ref, out_ref):
        hidden = jnp.maximum(dot(rows_ref[...], in_ref[0]), 0.0).astype(BF16)
        return dot(hidden, out_ref[0])

    @pl.when(k == 0)
    def _():
        total_ref[...] = term(in0_ref, out0_ref)

    @pl.when((k > 0) & (k < steps))
    def _():
        total_ref[...] += term(in0_ref, out0_ref)

    @pl.when((k >= steps) & (k < 2 * steps - 1))
    def _():
        total_ref[...] += term(in1_ref, out1_ref)

    @pl.when(k == 2 * steps - 1)
    def _():
        part_ref[...] = (total_ref[...] + term(in1_ref, out1_ref)).astype(part_ref.dtype)


def expert(rows, w_in, w_out, other, j, dtype):
    room, wide = rows.shape
    half = other.shape[0] // 2
    hid = w_in.shape[2]
    steps = 2
    piece = hid // steps
    own, theirs = lambda k: jnp.minimum(k, steps - 1), lambda k: jnp.maximum(k - steps, 0)
    return pl.pallas_call(
        functools.partial(expert_kernel, steps),
        out_shape=jax.ShapeDtypeStruct((room, wide), dtype),
        grid=(2 * steps,),
        in_specs=[
            pl.BlockSpec((room, wide), lambda k: (0, 0)),
            pl.BlockSpec((1, wide, piece), lambda k: (j, 0, own(k))),
            pl.BlockSpec((1, piece, wide), lambda k: (j, own(k), 0)),
            pl.BlockSpec((1, wide, piece), lambda k: (j % half, 0, theirs(k))),
            pl.BlockSpec((1, piece, wide), lambda k: (half + j % half, theirs(k), 0)),
        ],
        out_specs=pl.BlockSpec((room, wide), lambda k: (0, 0)),
        scratch_shapes=[pltpu.VMEM((room, wide), F32)],
        compiler_params=params(),
        cost_estimate=cost(8 * room * wide * hid, 8 * wide * hid + 6 * room * wide),
        name="expert",
    )(rows, w_in, w_out, other, other)


def back_kernel(held, col_ref, *refs):
    own, other, out_ref = refs[:held], refs[held : 2 * held], refs[2 * held]
    rows = out_ref.shape[0]
    col = col_ref[:, 0:1].astype(jnp.int32)
    total = None
    for j in range(held):
        value = (own[j][...] + other[j][...].astype(F32)).astype(BF16)
        pick = ones_where(col - j * ROOM == iota((rows, ROOM), 1))
        part = dot(pick, value)
        total = part if total is None else total + part
    out_ref[...] = total.astype(BF16)


def back(col, own, other):
    held = len(own)
    total, wide = col.shape[0], own[0].shape[1]
    block = 512
    whole = pl.BlockSpec((ROOM, wide), lambda i: (0, 0))
    return pl.pallas_call(
        functools.partial(back_kernel, held),
        out_shape=jax.ShapeDtypeStruct((total, wide), BF16),
        grid=(total // block,),
        in_specs=[pl.BlockSpec((block, 128), lambda i: (i, 0))] + [whole] * (2 * held),
        out_specs=pl.BlockSpec((block, wide), lambda i: (i, 0)),
        compiler_params=params(),
        cost_estimate=cost(2 * total * held * ROOM * wide, 8 * total * wide),
        name="back",
    )(col, *own, *other)


def combine_kernel(col_ref, returned_ref, out_ref):
    rows, total = out_ref.shape[0], returned_ref.shape[0]
    col = col_ref[:, 0:1].astype(jnp.int32)
    gate = col_ref[:, 1:2]
    pick = ones_where(col == iota((rows, total), 1))
    out_ref[...] = (gate * dot(pick, returned_ref[...])).astype(BF16)


def combine(col, returned):
    toks = col.shape[0]
    total, wide = returned.shape
    block = 256
    return pl.pallas_call(
        combine_kernel,
        out_shape=jax.ShapeDtypeStruct((toks, wide), BF16),
        grid=(toks // block,),
        in_specs=[
            pl.BlockSpec((block, 128), lambda i: (i, 0)),
            pl.BlockSpec((total, wide), lambda i: (0, 0)),
        ],
        out_specs=pl.BlockSpec((block, wide), lambda i: (i, 0)),
        compiler_params=params(),
        cost_estimate=cost(2 * total * toks * wide, 4 * total * wide),
        name="combine",
    )(col, returned)


def assign(first, backup, capacity, count, slot):
    columns = jnp.arange(count, dtype=jnp.int32)
    where = jnp.arange(first.shape[0], dtype=jnp.int32)
    earlier = ones_where(where[None, :] < where[:, None])
    onehot = (first[:, None] == columns[None, :]).astype(F32)
    rank = jnp.sum(dot(earlier, onehot.astype(BF16)) * onehot, axis=1)
    limit = jnp.sum(onehot * capacity[None, :].astype(F32), axis=1)
    kept = rank < limit
    spill = jnp.where((backup[:, None] == columns[None, :]) & ~kept[:, None], 1.0, 0.0)
    spill_rank = jnp.sum(dot(earlier, spill.astype(BF16)) * spill, axis=1)
    final = jnp.where(kept, first, backup)
    slots = jnp.where(kept, rank, slot + spill_rank).astype(jnp.int32)
    return slots, final


def general(tokens, gate, first, backup, capacity, w_in, w_out):
    held = w_in.shape[0]
    owners = lax.axis_size(EXPERT)
    helpers = lax.axis_size("helper")
    experts = held * owners
    slot = max(6, 3 * tokens.shape[0] // (2 * experts))
    slots, final = assign(first, backup, capacity, experts, slot)
    wide = tokens.shape[1]
    buffer = jnp.zeros((experts, 2 * slot, wide), BF16).at[final, slots].set(tokens)
    buffer = buffer.reshape(owners, held * 2 * slot, wide)
    arrived = lax.all_to_all(buffer, EXPERT, 0, 0, tiled=True)
    arrived = arrived.reshape(owners, held, 2 * slot, wide)
    whole_in = lax.all_gather(w_in, "helper", axis=2, tiled=True)
    whole_out = lax.all_gather(w_out, "helper", axis=1, tiled=True)
    width = whole_in.shape[2] // helpers
    outputs = []
    for e in range(held):
        rows = arrived[:, e].reshape(owners * 2 * slot, wide)
        total = jnp.zeros(rows.shape, F32)
        for q in range(helpers):
            part = slice(q * width, (q + 1) * width)
            hidden = jnp.maximum(dot(rows, whole_in[e, :, part]), 0.0).astype(BF16)
            total = total + dot(hidden, whole_out[e, part, :]).astype(BF16).astype(F32)
        outputs.append(total.astype(BF16).reshape(owners, 2 * slot, wide))
    result = jnp.stack(outputs, axis=1).reshape(owners, held * 2 * slot, wide)
    returned = lax.all_to_all(result, EXPERT, 0, 0, tiled=True)
    picked = returned.reshape(experts, 2 * slot, wide)[final, slots]
    return (gate[:, None] * picked.astype(F32)).astype(BF16)


def on_device(tokens, gate, expert_ids, backup_ids, capacity, w_in, w_out):
    held = w_in.shape[0]
    owners = lax.axis_size(EXPERT)
    helpers = lax.axis_size("helper")
    toks, wide = tokens.shape
    half = held // 2
    pairs = [PAIR_A if j < half else PAIR_B for j in range(held)]
    cross = [PAIR_B if j < half else PAIR_A for j in range(held)]
    order = [k for i in range(half) for k in (i, i + half)]
    group = lax.axis_index(EXPERT).astype(jnp.int32).reshape(1)
    pieces = [jnp.concatenate([w_in[k : k + half], w_out[k : k + half]]) for k in (0, half)]
    pieces, expert_ids = lax.optimization_barrier((pieces, expert_ids))
    other = [lax.ppermute(p, "helper", pairs[k * half]) for k, p in enumerate(pieces)]
    row, col, count = route(
        expert_ids.reshape(1, toks),
        backup_ids.reshape(1, toks),
        capacity.reshape(1, -1),
        gate.reshape(1, toks),
        held,
    )
    counts = lax.all_gather(count, EXPERT, axis=0, tiled=True)
    row, counts = lax.optimization_barrier((row, counts))
    bins = pick(row, tokens, 0, owners * BIN, 4, "dispatch")
    arrived = lax.all_to_all(bins.reshape(owners, BIN, wide), EXPERT, 0, 0, tiled=True)
    arrived = arrived.reshape(owners * BIN, wide)
    place_row, place_col, over = places(group, counts, held)
    overs = [over] + [
        lax.ppermute(over, "helper", [(i, (i + k) % helpers) for i in range(helpers)])
        for k in range(1, helpers)
    ]
    rows, theirs = {}, {}
    for j in order:
        rows[j] = pick(place_row, arrived, j * ROOM, ROOM, 1, "regroup")
        theirs[j] = lax.ppermute(rows[j], "helper", cross[j])
    own, sent = {}, {}
    for j in order:
        args = (w_in, w_out, other[j // half], j)
        own[j] = expert(rows[j], *args, F32)
        sent[j] = lax.ppermute(expert(theirs[j], *args, BF16), "helper", cross[j])
    result = back(place_col, [own[j] for j in range(held)], [sent[j] for j in range(held)])
    returned = lax.all_to_all(result.reshape(owners, BIN, wide), EXPERT, 0, 0, tiled=True)
    mixed = combine(col, returned.reshape(owners * BIN, wide))
    return lax.cond(
        functools.reduce(jnp.maximum, [o[0, 0] for o in overs]) > 0,
        lambda ops: general(*ops[1:]),
        lambda ops: ops[0],
        (mixed, tokens, gate, expert_ids[:, 0], backup_ids[:, 0], capacity, w_in, w_out),
    )


def solution(mesh):
    torus = Mesh(
        mesh.devices.reshape(4, 4, 2, mesh.shape["helper"]),
        ("expert_0", "expert_1", "expert_2", "helper"),
    )
    in_specs = (
        P(EXPERT_HELPER, None),
        P(EXPERT_HELPER),
        P(EXPERT_HELPER, None),
        P(EXPERT_HELPER, None),
        P(),
        P(EXPERT, None, "helper"),
        P(EXPERT, "helper", None),
    )
    out_specs = P(EXPERT_HELPER, None)
    return jax.shard_map(
        on_device, mesh=torus, in_specs=in_specs, out_specs=out_specs, check_vma=False
    )
```

```python
import functools

import jax
import jax.numpy as jnp
from jax import lax
from jax.experimental import pallas as pl
from jax.experimental.pallas import tpu as pltpu
from jax.sharding import Mesh
from jax.sharding import PartitionSpec as P

EXPERT = ("expert_0", "expert_1", "expert_2")
EXPERT_HELPER = ("expert_0", "expert_1", "expert_2", "helper")
CHUNK = 2
BIN = 40
ROOM = 544
CORE_X = ("expert_2", "helper")
NEAR = [(0, 1), (1, 0), (2, 3), (3, 2), (5, 6), (6, 5), (7, 4), (4, 7)]
FAR = [(1, 2), (2, 1), (3, 0), (0, 3), (4, 5), (5, 4), (6, 7), (7, 6)]
F32 = jnp.float32
BF16 = jnp.bfloat16
VMEM_LIMIT = 24 * 1024 * 1024


def dot(a, b):
    return jnp.dot(a, b, preferred_element_type=F32)


def dot_nt(a, b):
    return lax.dot_general(a, b, (((1,), (1,)), ((), ())), preferred_element_type=F32)


def iota(shape, dim):
    return lax.broadcasted_iota(jnp.int32, shape, dim)


def ones_where(cond):
    return jnp.where(cond, 1.0, 0.0).astype(BF16)


def params():
    return pltpu.CompilerParams(vmem_limit_bytes=VMEM_LIMIT)


def cost(flops, read):
    return pl.CostEstimate(flops=flops, bytes_accessed=read, transcendentals=0)


def route_kernel(held, first_ref, backup_ref, cap_ref, gate_ref, row_ref, col_ref, meta_ref):
    count = cap_ref.shape[1]
    toks = first_ref.shape[1]
    chunks = held // CHUNK
    ids = iota((count, toks), 0)
    first = first_ref[...]
    backup = backup_ref[...]
    one = jnp.where(ids == first, 1.0, 0.0)
    two = jnp.where(ids == backup, 1.0, 0.0)
    earlier = ones_where(iota((toks, toks), 0) < iota((toks, toks), 1))
    rank = jnp.sum(dot(one.astype(BF16), earlier) * one, axis=0, keepdims=True)
    cap = jnp.broadcast_to(cap_ref[...].astype(F32), (8, count)).astype(BF16)
    limit = dot(cap, one.astype(BF16))[0:1]
    kept = jnp.where(rank < limit, 1.0, 0.0)
    spill = two * (1.0 - kept)
    spill_rank = jnp.sum(dot(spill.astype(BF16), earlier) * spill, axis=0, keepdims=True)
    mine = one * kept
    n_kept = jnp.sum(mine, axis=1, keepdims=True)
    final = mine + spill
    n_all = jnp.sum(final, axis=1, keepdims=True)
    e0, e1 = iota((count, count), 0), iota((count, count), 1)
    wide = jnp.broadcast_to(n_all, (count, count)).astype(BF16)
    start = dot(ones_where((e1 < e0) & (e1 // CHUNK == e0 // CHUNK)), wide)
    fullest = jnp.max(dot(ones_where(e1 // CHUNK == e0 // CHUNK), wide))
    over = jnp.where(fullest > BIN - 1, 1.0, 0.0)
    for c in range(chunks):
        here = e0 % held // CHUNK == c
        value = jnp.where(e1 == e0 % CHUNK, n_all, jnp.where(e1 == CHUNK, over, 0.0))
        meta_ref[c] = jnp.where(here, value, 0.0).astype(BF16)
    place = jnp.sum(final * start[:, 0:1] + spill * n_kept, axis=0, keepdims=True)
    place = place + jnp.where(kept > 0.5, rank, spill_rank)
    chosen = jnp.where(kept > 0.5, first, backup)
    bins = chosen % held // CHUNK * (count // held) + chosen // held
    row = jnp.where(place < BIN - 1, bins.astype(F32) * BIN + place, -1.0)
    row_ref[...] = jnp.broadcast_to(row, (8, toks)).astype(jnp.int32)
    stacked = jnp.where(
        iota((128, toks), 0) == 0,
        jnp.broadcast_to(row, (128, toks)),
        jnp.broadcast_to(gate_ref[...], (128, toks)),
    )
    col_ref[...] = stacked.T


def route(first, backup, capacity, gate, held):
    toks, count = first.shape[1], capacity.shape[1]
    return pl.pallas_call(
        functools.partial(route_kernel, held),
        out_shape=(
            jax.ShapeDtypeStruct((8, toks), jnp.int32),
            jax.ShapeDtypeStruct((toks, 128), F32),
            jax.ShapeDtypeStruct((held // CHUNK, count, count), BF16),
        ),
        compiler_params=params(),
        cost_estimate=cost(4 * toks * toks * count, toks * 512),
        name="route",
    )(first, backup, capacity, gate)


def dispatch_kernel(chunk, held, row_ref, tok_ref, meta_ref, out_ref):
    rows, toks = out_ref.shape[0], tok_ref.shape[0]
    count = meta_ref.shape[1]
    begin = pl.program_id(0) * rows
    at = iota((rows, toks), 0) + (begin + chunk * (count // held) * BIN)
    value = dot(ones_where(at == row_ref[0:1, :]), tok_ref[...])
    out_ref[...] = value.astype(BF16)
    at = iota((rows, count), 0) + begin
    spare = ones_where((at % BIN == BIN - 1) & (at // BIN == iota((rows, count), 1) // held))
    out_ref[:, 0:count] = (value[:, 0:count] + dot(spare, meta_ref[0])).astype(BF16)


def dispatch(row, tokens, meta, chunk, held):
    toks, wide = tokens.shape
    count = meta.shape[1]
    total = count // held * BIN
    block = total // 2
    return pl.pallas_call(
        functools.partial(dispatch_kernel, chunk, held),
        out_shape=jax.ShapeDtypeStruct((total, wide), BF16),
        grid=(total // block,),
        in_specs=[
            pl.BlockSpec((8, toks), lambda i: (0, 0)),
            pl.BlockSpec((toks, wide), lambda i: (0, 0)),
            pl.BlockSpec((1, count, count), lambda i: (chunk, 0, 0)),
        ],
        out_specs=pl.BlockSpec((block, wide), lambda i: (i, 0)),
        compiler_params=params(),
        cost_estimate=cost(2 * total * toks * wide, 2 * (total + toks) * wide),
        name="dispatch",
    )(row, tokens, meta)


def places_kernel(arrived_ref, row_ref, col_ref, over_ref):
    total = arrived_ref.shape[0]
    sources = total // BIN
    spare = ones_where(iota((sources, total), 1) == iota((sources, total), 0) * BIN + (BIN - 1))
    meta = dot(spare, arrived_ref[...]).astype(BF16)
    lane = ones_where(iota((8, 128), 0) == iota((8, 128), 1))
    told = dot_nt(lane, meta)
    n = jnp.where(iota((8, sources), 0) < CHUNK, told, 0.0)
    flagged = jnp.max(jnp.where(iota((8, sources), 0) == CHUNK, told, 0.0))
    busiest = jnp.max(jnp.sum(n, axis=1, keepdims=True))
    over = jnp.where((flagged > 0.5) | (busiest > ROOM), 1.0, 0.0)
    over_ref[...] = jnp.broadcast_to(over, (8, 128))
    base = dot(n.astype(BF16), ones_where(iota((sources, sources), 0) < iota((sources, sources), 1)))
    begin = jnp.zeros((8, sources), F32)
    for j in range(CHUNK):
        ahead = iota((8, sources), 0) > j
        begin = begin + jnp.where(ahead, jnp.broadcast_to(n[j : j + 1], (8, sources)), 0.0)
    shift = base - begin + 128.0
    high = jnp.floor(shift * (1.0 / 128.0))
    low = shift - high * 128.0
    spread = ones_where(iota((sources, total), 1) // BIN == iota((sources, total), 0))
    place = dot(high.astype(BF16), spread) * 128.0 + dot(low.astype(BF16), spread) - 128.0
    begin = dot(begin.astype(BF16), spread)
    end = begin + dot(n.astype(BF16), spread)
    r = (iota((8, total), 1) % BIN).astype(F32)
    place = place + r
    inside = (r >= begin) & (r < end) & (place < ROOM) & (r < BIN - 1)
    index = jnp.where(inside, place + iota((8, total), 0).astype(F32) * ROOM + 1.0, 0.0)
    index = jnp.sum(index, axis=0, keepdims=True) - 1.0
    row_ref[...] = jnp.broadcast_to(index, (8, total)).astype(jnp.int32)
    col_ref[...] = jnp.broadcast_to(index, (128, total)).T


def places(arrived):
    total = arrived.shape[0]
    return pl.pallas_call(
        places_kernel,
        out_shape=(
            jax.ShapeDtypeStruct((8, total), jnp.int32),
            jax.ShapeDtypeStruct((total, 128), F32),
            jax.ShapeDtypeStruct((8, 128), F32),
        ),
        grid=(1,),
        in_specs=[pl.BlockSpec((total, 128), lambda i: (0, 0))],
        out_specs=(
            pl.BlockSpec((8, total), lambda i: (0, 0)),
            pl.BlockSpec((total, 128), lambda i: (0, 0)),
            pl.BlockSpec((8, 128), lambda i: (0, 0)),
        ),
        compiler_params=params(),
        cost_estimate=cost(1 << 25, 1 << 19),
        name="places",
    )(arrived)


def regroup_kernel(index_ref, rows_ref, out_ref):
    count, many = out_ref.shape[0], rows_ref.shape[0]
    here = iota((count, many), 0) + pl.program_id(0) * count
    out_ref[...] = dot(ones_where(here == index_ref[0:1, :]), rows_ref[...]).astype(BF16)


def regroup(index, rows):
    many, wide = rows.shape
    return pl.pallas_call(
        regroup_kernel,
        out_shape=jax.ShapeDtypeStruct((CHUNK * ROOM, wide), BF16),
        grid=(CHUNK,),
        in_specs=[
            pl.BlockSpec((8, many), lambda i: (0, 0)),
            pl.BlockSpec((many, wide), lambda i: (0, 0)),
        ],
        out_specs=pl.BlockSpec((ROOM, wide), lambda i: (i, 0)),
        compiler_params=params(),
        cost_estimate=cost(2 * CHUNK * ROOM * many * wide, 2 * (CHUNK * ROOM + many) * wide),
        name="regroup",
    )(index, rows)


def expert_kernel(rows_ref, in_ref, out_ref, *refs):
    hidden = jnp.maximum(dot(rows_ref[...], in_ref[0]), 0.0).astype(BF16)
    part = dot(hidden, out_ref[0])
    if len(refs) == 2:
        part = part + refs[0][...]
    refs[-1][...] = part.astype(refs[-1].dtype)


def expert(rows, w_in, w_out, chunk, so_far, dtype):
    wide, hid = w_in.shape[1], w_in.shape[2]
    total = rows.shape[0]
    block = pl.BlockSpec((ROOM, wide), lambda i: (i, 0))
    extra = [] if so_far is None else [so_far]
    return pl.pallas_call(
        expert_kernel,
        out_shape=jax.ShapeDtypeStruct((total, wide), dtype),
        grid=(CHUNK,),
        in_specs=[
            block,
            pl.BlockSpec((1, wide, hid), lambda i: (chunk * CHUNK + i, 0, 0)),
            pl.BlockSpec((1, hid, wide), lambda i: (chunk * CHUNK + i, 0, 0)),
        ]
        + [block] * len(extra),
        out_specs=block,
        compiler_params=params(),
        cost_estimate=cost(4 * total * wide * hid, 4 * CHUNK * wide * hid + 6 * total * wide),
        name="expert",
    )(rows, w_in, w_out, *extra)


def back_kernel(col_ref, own_ref, sent_ref, over_ref, out_ref):
    rows, many = out_ref.shape[0], own_ref.shape[0]
    value = (own_ref[...] + sent_ref[...].astype(F32)).astype(BF16)
    col = col_ref[:, 0:1].astype(jnp.int32)
    result = dot(ones_where(col == iota((rows, many), 1)), value)
    out_ref[...] = result.astype(BF16)
    at = iota((rows, 128), 0) + pl.program_id(0) * rows
    flag = jnp.where(at % BIN == BIN - 1, over_ref[0:1, :], 0.0)
    out_ref[:, 0:128] = (result[:, 0:128] + flag).astype(BF16)


def back(col, own, sent, over):
    total, (many, wide) = col.shape[0], own.shape
    block = total // 2
    whole = pl.BlockSpec((many, wide), lambda i: (0, 0))
    return pl.pallas_call(
        back_kernel,
        out_shape=jax.ShapeDtypeStruct((total, wide), BF16),
        grid=(total // block,),
        in_specs=[
            pl.BlockSpec((block, 128), lambda i: (i, 0)),
            whole,
            whole,
            pl.BlockSpec((8, 128), lambda i: (0, 0)),
        ],
        out_specs=pl.BlockSpec((block, wide), lambda i: (i, 0)),
        compiler_params=params(),
        cost_estimate=cost(2 * total * many * wide, 2 * total * wide + 6 * many * wide),
        name="back",
    )(col, own, sent, over)


def combine_kernel(chunk, last, col_ref, returned_ref, *refs):
    rows, many = refs[-2].shape[0], returned_ref.shape[0]
    col = col_ref[:, 0:1].astype(jnp.int32)
    total = dot(ones_where(col - chunk * many == iota((rows, many), 1)), returned_ref[...])
    if chunk > 0:
        total = total + refs[0][...].astype(F32)
    if last:
        total = total * col_ref[:, 1:2]
    refs[-2][...] = total.astype(BF16)
    spare = iota((many, 128), 0) % BIN == BIN - 1
    over = jnp.max(jnp.where(spare, returned_ref[:, 0:128].astype(F32), 0.0))
    refs[-1][...] = jnp.broadcast_to(jnp.where(over > 0.5, 1, 0), (8, 128))


def combine(col, returned, chunk, last, so_far):
    toks, (many, wide) = col.shape[0], returned.shape
    block = toks // 2
    extra = [] if so_far is None else [so_far]
    return pl.pallas_call(
        functools.partial(combine_kernel, chunk, last),
        out_shape=(
            jax.ShapeDtypeStruct((toks, wide), BF16),
            jax.ShapeDtypeStruct((8, 128), jnp.int32),
        ),
        grid=(toks // block,),
        in_specs=[
            pl.BlockSpec((block, 128), lambda i: (i, 0)),
            pl.BlockSpec((many, wide), lambda i: (0, 0)),
        ]
        + [pl.BlockSpec((block, wide), lambda i: (i, 0))] * len(extra),
        out_specs=(
            pl.BlockSpec((block, wide), lambda i: (i, 0)),
            pl.BlockSpec((8, 128), lambda i: (0, 0)),
        ),
        compiler_params=params(),
        cost_estimate=cost(2 * toks * many * wide, 2 * (many + 2 * toks) * wide),
        name="combine",
    )(col, returned, *extra)


def assign(first, backup, capacity, count, slot):
    columns = jnp.arange(count, dtype=jnp.int32)
    where = jnp.arange(first.shape[0], dtype=jnp.int32)
    earlier = ones_where(where[None, :] < where[:, None])
    onehot = (first[:, None] == columns[None, :]).astype(F32)
    rank = jnp.sum(dot(earlier, onehot.astype(BF16)) * onehot, axis=1)
    limit = jnp.sum(onehot * capacity[None, :].astype(F32), axis=1)
    kept = rank < limit
    spill = jnp.where((backup[:, None] == columns[None, :]) & ~kept[:, None], 1.0, 0.0)
    spill_rank = jnp.sum(dot(earlier, spill.astype(BF16)) * spill, axis=1)
    final = jnp.where(kept, first, backup)
    slots = jnp.where(kept, rank, slot + spill_rank).astype(jnp.int32)
    return slots, final


def general(tokens, gate, first, backup, capacity, w_in, w_out):
    held = w_in.shape[0]
    owners = lax.axis_size(EXPERT)
    helpers = lax.axis_size("helper")
    experts = held * owners
    slot = max(6, 3 * tokens.shape[0] // (2 * experts))
    slots, final = assign(first, backup, capacity, experts, slot)
    wide = tokens.shape[1]
    buffer = jnp.zeros((experts, 2 * slot, wide), BF16).at[final, slots].set(tokens)
    buffer = buffer.reshape(owners, held * 2 * slot, wide)
    arrived = lax.all_to_all(buffer, EXPERT, 0, 0, tiled=True)
    arrived = arrived.reshape(owners, held, 2 * slot, wide)
    whole_in = lax.all_gather(w_in, "helper", axis=2, tiled=True)
    whole_out = lax.all_gather(w_out, "helper", axis=1, tiled=True)
    width = whole_in.shape[2] // helpers
    outputs = []
    for e in range(held):
        rows = arrived[:, e].reshape(owners * 2 * slot, wide)
        total = jnp.zeros(rows.shape, F32)
        for q in range(helpers):
            part = slice(q * width, (q + 1) * width)
            hidden = jnp.maximum(dot(rows, whole_in[e, :, part]), 0.0).astype(BF16)
            total = total + dot(hidden, whole_out[e, part, :]).astype(BF16).astype(F32)
        outputs.append(total.astype(BF16).reshape(owners, 2 * slot, wide))
    result = jnp.stack(outputs, axis=1).reshape(owners, held * 2 * slot, wide)
    returned = lax.all_to_all(result, EXPERT, 0, 0, tiled=True)
    picked = returned.reshape(experts, 2 * slot, wide)[final, slots]
    return (gate[:, None] * picked.astype(F32)).astype(BF16)


def after(*values):
    return lax.optimization_barrier(values)


def on_device(tokens, gate, expert_ids, backup_ids, capacity, w_in, w_out):
    held = w_in.shape[0]
    owners = lax.axis_size(EXPERT)
    helpers = lax.axis_size("helper")
    toks, wide = tokens.shape
    chunks = range(held // CHUNK)
    other_in = lax.ppermute(w_in, CORE_X, NEAR)
    other_out = lax.ppermute(w_out, CORE_X, NEAR)
    row, col, meta = route(
        expert_ids.reshape(1, toks),
        backup_ids.reshape(1, toks),
        capacity.reshape(1, -1),
        gate.reshape(1, toks),
        held,
    )

    def exchange(rows):
        rows = lax.all_to_all(rows.reshape(owners, BIN, wide), EXPERT, 0, 0, tiled=True)
        return rows.reshape(owners * BIN, wide)

    arrived = [exchange(dispatch(row, tokens, meta, c, held)) for c in chunks]
    at_row, at_col, overs = zip(*[places(a) for a in arrived])
    rows = [regroup(at_row[c], arrived[c]) for c in chunks]
    theirs = [lax.ppermute(rows[c], CORE_X, FAR) for c in chunks]
    over = functools.reduce(jnp.maximum, overs)
    around = [[(i, (i + k) % helpers) for i in range(helpers)] for k in range(1, helpers)]
    over = functools.reduce(jnp.maximum, [over] + [lax.ppermute(over, "helper", a) for a in around])
    own = [expert(rows[c], w_in, w_out, c, None, F32) for c in chunks]
    theirs, own = zip(*[after(theirs[c], own[c]) for c in chunks])
    made = [expert(theirs[c], w_in, w_out, c, None, F32) for c in chunks]
    made = [expert(theirs[c], other_in, other_out, c, made[c], BF16) for c in chunks]
    sent = [lax.ppermute(made[c], CORE_X, FAR) for c in chunks]
    own, made = after(list(own), made)
    own = [expert(rows[c], other_in, other_out, c, own[c], F32) for c in chunks]
    mixed = None
    for c in chunks:
        last = c == chunks[-1]
        returned = exchange(back(at_col[c], own[c], sent[c], over))
        mixed, general_too = combine(col, returned, c, last, mixed)
    return lax.cond(
        general_too[0, 0] > 0,
        lambda ops: general(*ops[1:]),
        lambda ops: ops[0],
        (mixed, tokens, gate, expert_ids[:, 0], backup_ids[:, 0], capacity, w_in, w_out),
    )


def solution(mesh):
    torus = Mesh(
        mesh.devices.reshape(4, 4, 2, mesh.shape["helper"]),
        ("expert_0", "expert_1", "expert_2", "helper"),
    )
    in_specs = (
        P(EXPERT_HELPER, None),
        P(EXPERT_HELPER),
        P(EXPERT_HELPER, None),
        P(EXPERT_HELPER, None),
        P(),
        P(EXPERT, None, "helper"),
        P(EXPERT, "helper", None),
    )
    out_specs = P(EXPERT_HELPER, None)
    return jax.shard_map(
        on_device, mesh=torus, in_specs=in_specs, out_specs=out_specs, check_vma=False
    )
```

```python
import functools

import jax
import jax.numpy as jnp
from jax import lax
from jax.experimental import pallas as pl
from jax.experimental.pallas import tpu as pltpu
from jax.sharding import Mesh
from jax.sharding import PartitionSpec as P

EXPERT = ("expert_0", "expert_1", "expert_2")
EXPERT_HELPER = ("expert_0", "expert_1", "expert_2", "helper")
CHUNK = 2
BIN = 40
ROOM = 544
CORE_X = ("expert_2", "helper")
NEAR = [(0, 1), (1, 0), (2, 3), (3, 2), (5, 6), (6, 5), (7, 4), (4, 7)]
FAR = [(1, 2), (2, 1), (3, 0), (0, 3), (4, 5), (5, 4), (6, 7), (7, 6)]
F32 = jnp.float32
BF16 = jnp.bfloat16
VMEM_LIMIT = 24 * 1024 * 1024
VMEM_ALL = 60 * 1024 * 1024


def dot(a, b):
    return jnp.dot(a, b, preferred_element_type=F32)


def dot_nt(a, b):
    return lax.dot_general(a, b, (((1,), (1,)), ((), ())), preferred_element_type=F32)


def iota(shape, dim):
    return lax.broadcasted_iota(jnp.int32, shape, dim)


def ones_where(cond):
    return jnp.where(cond, 1.0, 0.0).astype(BF16)


def params(limit=VMEM_LIMIT):
    return pltpu.CompilerParams(vmem_limit_bytes=limit)


def cost(flops, read):
    return pl.CostEstimate(flops=flops // 8, bytes_accessed=read // 8, transcendentals=0)


def route_kernel(held, first_ref, backup_ref, cap_ref, gate_ref, row_ref, col_ref, meta_ref):
    count = cap_ref.shape[1]
    toks = first_ref.shape[1]
    chunks = held // CHUNK
    ids = iota((count, toks), 0)
    first = first_ref[...]
    backup = backup_ref[...]
    one = jnp.where(ids == first, 1.0, 0.0)
    two = jnp.where(ids == backup, 1.0, 0.0)
    earlier = ones_where(iota((toks, toks), 0) < iota((toks, toks), 1))
    rank = jnp.sum(dot(one.astype(BF16), earlier) * one, axis=0, keepdims=True)
    cap = jnp.broadcast_to(cap_ref[...].astype(F32), (8, count)).astype(BF16)
    limit = dot(cap, one.astype(BF16))[0:1]
    kept = jnp.where(rank < limit, 1.0, 0.0)
    spill = two * (1.0 - kept)
    spill_rank = jnp.sum(dot(spill.astype(BF16), earlier) * spill, axis=0, keepdims=True)
    mine = one * kept
    n_kept = jnp.sum(mine, axis=1, keepdims=True)
    final = mine + spill
    n_all = jnp.sum(final, axis=1, keepdims=True)
    e0, e1 = iota((count, count), 0), iota((count, count), 1)
    wide = jnp.broadcast_to(n_all, (count, count)).astype(BF16)
    start = dot(ones_where((e1 < e0) & (e1 // CHUNK == e0 // CHUNK)), wide)
    fullest = jnp.max(dot(ones_where(e1 // CHUNK == e0 // CHUNK), wide))
    over = jnp.where(fullest > BIN - 1, 1.0, 0.0)
    for c in range(chunks):
        here = e0 % held // CHUNK == c
        value = jnp.where(e1 == e0 % CHUNK, n_all, jnp.where(e1 == CHUNK, over, 0.0))
        meta_ref[c] = jnp.where(here, value, 0.0).astype(BF16)
    place = jnp.sum(final * start[:, 0:1] + spill * n_kept, axis=0, keepdims=True)
    place = place + jnp.where(kept > 0.5, rank, spill_rank)
    chosen = jnp.where(kept > 0.5, first, backup)
    bins = chosen % held // CHUNK * (count // held) + chosen // held
    row = jnp.where(place < BIN - 1, bins.astype(F32) * BIN + place, -1.0)
    row_ref[...] = jnp.broadcast_to(row, (8, toks)).astype(jnp.int32)
    stacked = jnp.where(
        iota((128, toks), 0) == 0,
        jnp.broadcast_to(row, (128, toks)),
        jnp.broadcast_to(gate_ref[...], (128, toks)),
    )
    col_ref[...] = stacked.T


def route(first, backup, capacity, gate, held):
    toks, count = first.shape[1], capacity.shape[1]
    return pl.pallas_call(
        functools.partial(route_kernel, held),
        out_shape=(
            jax.ShapeDtypeStruct((8, toks), jnp.int32),
            jax.ShapeDtypeStruct((toks, 128), F32),
            jax.ShapeDtypeStruct((held // CHUNK, count, count), BF16),
        ),
        compiler_params=params(),
        cost_estimate=cost(4 * toks * toks * count, toks * 512),
        name="route",
    )(first, backup, capacity, gate)


def dispatch_kernel(chunk, held, row_ref, tok_ref, meta_ref, out_ref):
    rows, toks = out_ref.shape[0], tok_ref.shape[0]
    count = meta_ref.shape[1]
    begin = pl.program_id(0) * rows
    at = iota((rows, toks), 0) + (begin + chunk * (count // held) * BIN)
    value = dot(ones_where(at == row_ref[0:1, :]), tok_ref[...])
    out_ref[...] = value.astype(BF16)
    at = iota((rows, count), 0) + begin
    spare = ones_where((at % BIN == BIN - 1) & (at // BIN == iota((rows, count), 1) // held))
    out_ref[:, 0:count] = (value[:, 0:count] + dot(spare, meta_ref[0])).astype(BF16)


def dispatch(row, tokens, meta, chunk, held):
    toks, wide = tokens.shape
    count = meta.shape[1]
    total = count // held * BIN
    block = total // 2
    return pl.pallas_call(
        functools.partial(dispatch_kernel, chunk, held),
        out_shape=jax.ShapeDtypeStruct((total, wide), BF16),
        grid=(total // block,),
        in_specs=[
            pl.BlockSpec((8, toks), lambda i: (0, 0)),
            pl.BlockSpec((toks, wide), lambda i: (0, 0)),
            pl.BlockSpec((1, count, count), lambda i: (chunk, 0, 0)),
        ],
        out_specs=pl.BlockSpec((block, wide), lambda i: (i, 0)),
        compiler_params=params(VMEM_ALL),
        cost_estimate=cost(2 * total * toks * wide, 2 * (total + toks) * wide),
        name="dispatch",
    )(row, tokens, meta)


def places_kernel(arrived_ref, row_ref, col_ref, over_ref):
    total = arrived_ref.shape[0]
    sources = total // BIN
    spare = ones_where(iota((sources, total), 1) == iota((sources, total), 0) * BIN + (BIN - 1))
    meta = dot(spare, arrived_ref[...]).astype(BF16)
    lane = ones_where(iota((8, 128), 0) == iota((8, 128), 1))
    told = dot_nt(lane, meta)
    n = jnp.where(iota((8, sources), 0) < CHUNK, told, 0.0)
    flagged = jnp.max(jnp.where(iota((8, sources), 0) == CHUNK, told, 0.0))
    busiest = jnp.max(jnp.sum(n, axis=1, keepdims=True))
    over = jnp.where((flagged > 0.5) | (busiest > ROOM), 1.0, 0.0)
    over_ref[...] = jnp.broadcast_to(over, (8, 128))
    base = dot(n.astype(BF16), ones_where(iota((sources, sources), 0) < iota((sources, sources), 1)))
    begin = jnp.zeros((8, sources), F32)
    for j in range(CHUNK):
        ahead = iota((8, sources), 0) > j
        begin = begin + jnp.where(ahead, jnp.broadcast_to(n[j : j + 1], (8, sources)), 0.0)
    shift = base - begin + 128.0
    high = jnp.floor(shift * (1.0 / 128.0))
    low = shift - high * 128.0
    spread = ones_where(iota((sources, total), 1) // BIN == iota((sources, total), 0))
    place = dot(high.astype(BF16), spread) * 128.0 + dot(low.astype(BF16), spread) - 128.0
    begin = dot(begin.astype(BF16), spread)
    end = begin + dot(n.astype(BF16), spread)
    r = (iota((8, total), 1) % BIN).astype(F32)
    place = place + r
    inside = (r >= begin) & (r < end) & (place < ROOM) & (r < BIN - 1)
    index = jnp.where(inside, place + iota((8, total), 0).astype(F32) * ROOM + 1.0, 0.0)
    index = jnp.sum(index, axis=0, keepdims=True) - 1.0
    row_ref[...] = jnp.broadcast_to(index, (8, total)).astype(jnp.int32)
    col_ref[...] = jnp.broadcast_to(index, (128, total)).T


def places(arrived):
    total = arrived.shape[0]
    return pl.pallas_call(
        places_kernel,
        out_shape=(
            jax.ShapeDtypeStruct((8, total), jnp.int32),
            jax.ShapeDtypeStruct((total, 128), F32),
            jax.ShapeDtypeStruct((8, 128), F32),
        ),
        grid=(1,),
        in_specs=[pl.BlockSpec((total, 128), lambda i: (0, 0))],
        out_specs=(
            pl.BlockSpec((8, total), lambda i: (0, 0)),
            pl.BlockSpec((total, 128), lambda i: (0, 0)),
            pl.BlockSpec((8, 128), lambda i: (0, 0)),
        ),
        compiler_params=params(),
        cost_estimate=cost(1 << 25, 1 << 19),
        name="places",
    )(arrived)


def regroup_kernel(index_ref, rows_ref, out_ref):
    count, many = out_ref.shape[0], rows_ref.shape[0]
    here = iota((count, many), 0) + pl.program_id(0) * count
    out_ref[...] = dot(ones_where(here == index_ref[0:1, :]), rows_ref[...]).astype(BF16)


def regroup(index, rows):
    many, wide = rows.shape
    return pl.pallas_call(
        regroup_kernel,
        out_shape=jax.ShapeDtypeStruct((CHUNK * ROOM, wide), BF16),
        grid=(CHUNK,),
        in_specs=[
            pl.BlockSpec((8, many), lambda i: (0, 0)),
            pl.BlockSpec((many, wide), lambda i: (0, 0)),
        ],
        out_specs=pl.BlockSpec((ROOM, wide), lambda i: (i, 0)),
        compiler_params=params(),
        cost_estimate=cost(2 * CHUNK * ROOM * many * wide, 2 * (CHUNK * ROOM + many) * wide),
        name="regroup",
    )(index, rows)


def weights_kernel(in_ref, out_ref, both_ref):
    @pl.when(pl.program_id(0) < CHUNK)
    def _():
        both_ref[...] = in_ref[...]

    @pl.when(pl.program_id(0) >= CHUNK)
    def _():
        both_ref[...] = out_ref[...]


def weights(w_in, w_out, first):
    _, wide, hid = w_in.shape
    return pl.pallas_call(
        weights_kernel,
        out_shape=jax.ShapeDtypeStruct((2 * CHUNK, wide, hid), w_in.dtype),
        grid=(2 * CHUNK,),
        in_specs=[
            pl.BlockSpec((1, wide, hid), lambda i: (first + jnp.minimum(i, CHUNK - 1), 0, 0)),
            pl.BlockSpec((1, hid, wide), lambda i: (first + jnp.maximum(i - CHUNK, 0), 0, 0)),
        ],
        out_specs=pl.BlockSpec((1, wide, hid), lambda i: (i, 0, 0)),
        compiler_params=params(VMEM_ALL),
        cost_estimate=cost(1, 8 * CHUNK * wide * hid),
        name="weights",
    )(w_in, w_out)


def expert_kernel(rows_ref, in_ref, out_ref, *refs):
    hidden = jnp.maximum(dot(rows_ref[...], in_ref[0]), 0.0).astype(BF16)
    part = dot(hidden, out_ref[0])
    if len(refs) == 2:
        part = part + refs[0][...]
    refs[-1][...] = part.astype(refs[-1].dtype)


def expert(rows, w_in, w_out, at_in, at_out, so_far, dtype):
    wide, hid = w_in.shape[1], w_in.shape[2]
    total = rows.shape[0]
    block = pl.BlockSpec((ROOM, wide), lambda i: (i, 0))
    extra = [] if so_far is None else [so_far]
    return pl.pallas_call(
        expert_kernel,
        out_shape=jax.ShapeDtypeStruct((total, wide), dtype),
        grid=(CHUNK,),
        in_specs=[
            block,
            pl.BlockSpec((1, wide, hid), lambda i: (at_in + i, 0, 0)),
            pl.BlockSpec((1, hid, wide), lambda i: (at_out + i, 0, 0)),
        ]
        + [block] * len(extra),
        out_specs=block,
        compiler_params=params(),
        cost_estimate=cost(4 * total * wide * hid, 4 * CHUNK * wide * hid + 6 * total * wide),
        name="expert",
    )(rows, w_in, w_out, *extra)


def back_kernel(col_ref, own_ref, sent_ref, over_ref, out_ref):
    rows, many = out_ref.shape[0], own_ref.shape[0]
    value = (own_ref[...] + sent_ref[...].astype(F32)).astype(BF16)
    col = col_ref[:, 0:1].astype(jnp.int32)
    result = dot(ones_where(col == iota((rows, many), 1)), value)
    out_ref[...] = result.astype(BF16)
    at = iota((rows, 128), 0) + pl.program_id(0) * rows
    flag = jnp.where(at % BIN == BIN - 1, over_ref[0:1, :], 0.0)
    out_ref[:, 0:128] = (result[:, 0:128] + flag).astype(BF16)


def back(col, own, sent, over):
    total, (many, wide) = col.shape[0], own.shape
    block = total // 2
    whole = pl.BlockSpec((many, wide), lambda i: (0, 0))
    return pl.pallas_call(
        back_kernel,
        out_shape=jax.ShapeDtypeStruct((total, wide), BF16),
        grid=(total // block,),
        in_specs=[
            pl.BlockSpec((block, 128), lambda i: (i, 0)),
            whole,
            whole,
            pl.BlockSpec((8, 128), lambda i: (0, 0)),
        ],
        out_specs=pl.BlockSpec((block, wide), lambda i: (i, 0)),
        compiler_params=params(VMEM_ALL),
        cost_estimate=cost(2 * total * many * wide, 2 * total * wide + 6 * many * wide),
        name="back",
    )(col, own, sent, over)


def combine_kernel(chunk, last, col_ref, returned_ref, *refs):
    rows, many = refs[-2].shape[0], returned_ref.shape[0]
    col = col_ref[:, 0:1].astype(jnp.int32)
    total = dot(ones_where(col - chunk * many == iota((rows, many), 1)), returned_ref[...])
    if chunk > 0:
        total = total + refs[0][...].astype(F32)
    if last:
        total = total * col_ref[:, 1:2]
    refs[-2][...] = total.astype(BF16)
    spare = iota((many, 128), 0) % BIN == BIN - 1
    over = jnp.max(jnp.where(spare, returned_ref[:, 0:128].astype(F32), 0.0))
    refs[-1][...] = jnp.broadcast_to(over, (8, 128))


def combine(col, returned, chunk, last, so_far):
    toks, (many, wide) = col.shape[0], returned.shape
    block = toks // 2
    extra = [] if so_far is None else [so_far]
    return pl.pallas_call(
        functools.partial(combine_kernel, chunk, last),
        out_shape=(
            jax.ShapeDtypeStruct((toks, wide), BF16),
            jax.ShapeDtypeStruct((8, 128), F32),
        ),
        grid=(toks // block,),
        in_specs=[
            pl.BlockSpec((block, 128), lambda i: (i, 0)),
            pl.BlockSpec((many, wide), lambda i: (0, 0)),
        ]
        + [pl.BlockSpec((block, wide), lambda i: (i, 0))] * len(extra),
        out_specs=(
            pl.BlockSpec((block, wide), lambda i: (i, 0)),
            pl.BlockSpec((8, 128), lambda i: (0, 0)),
        ),
        compiler_params=params(),
        cost_estimate=cost(2 * toks * many * wide, 2 * (many + 2 * toks) * wide),
        name="combine",
    )(col, returned, *extra)


def assign(first, backup, capacity, count, slot):
    columns = jnp.arange(count, dtype=jnp.int32)
    where = jnp.arange(first.shape[0], dtype=jnp.int32)
    earlier = ones_where(where[None, :] < where[:, None])
    onehot = (first[:, None] == columns[None, :]).astype(F32)
    rank = jnp.sum(dot(earlier, onehot.astype(BF16)) * onehot, axis=1)
    limit = jnp.sum(onehot * capacity[None, :].astype(F32), axis=1)
    kept = rank < limit
    spill = jnp.where((backup[:, None] == columns[None, :]) & ~kept[:, None], 1.0, 0.0)
    spill_rank = jnp.sum(dot(earlier, spill.astype(BF16)) * spill, axis=1)
    final = jnp.where(kept, first, backup)
    slots = jnp.where(kept, rank, slot + spill_rank).astype(jnp.int32)
    return slots, final


def general(tokens, gate, first, backup, capacity, w_in, w_out):
    held = w_in.shape[0]
    owners = lax.axis_size(EXPERT)
    helpers = lax.axis_size("helper")
    experts = held * owners
    slot = max(6, 3 * tokens.shape[0] // (2 * experts))
    slots, final = assign(first, backup, capacity, experts, slot)
    wide = tokens.shape[1]
    buffer = jnp.zeros((experts, 2 * slot, wide), BF16).at[final, slots].set(tokens)
    buffer = buffer.reshape(owners, held * 2 * slot, wide)
    arrived = lax.all_to_all(buffer, EXPERT, 0, 0, tiled=True)
    arrived = arrived.reshape(owners, held, 2 * slot, wide)
    rows = [arrived[:, e].reshape(owners * 2 * slot, wide) for e in range(held)]
    totals = [jnp.zeros(r.shape, F32) for r in rows]
    for k in range(helpers):
        turn = [(i, (i + k) % helpers) for i in range(helpers)]
        some_in = lax.ppermute(w_in, "helper", turn) if k else w_in
        some_out = lax.ppermute(w_out, "helper", turn) if k else w_out
        for e in range(held):
            hidden = jnp.maximum(dot(rows[e], some_in[e]), 0.0).astype(BF16)
            totals[e] = totals[e] + dot(hidden, some_out[e]).astype(BF16).astype(F32)
    outputs = [t.astype(BF16).reshape(owners, 2 * slot, wide) for t in totals]
    result = jnp.stack(outputs, axis=1).reshape(owners, held * 2 * slot, wide)
    returned = lax.all_to_all(result, EXPERT, 0, 0, tiled=True)
    picked = returned.reshape(experts, 2 * slot, wide)[final, slots]
    return (gate[:, None] * picked.astype(F32)).astype(BF16)


def after(*values):
    return lax.optimization_barrier(values)


def on_device(tokens, gate, expert_ids, backup_ids, capacity, w_in, w_out):
    held = w_in.shape[0]
    owners = lax.axis_size(EXPERT)
    helpers = lax.axis_size("helper")
    toks, wide = tokens.shape
    chunks = range(held // CHUNK)
    w_parts = [weights(w_in, w_out, c * CHUNK) for c in chunks]
    others = [lax.ppermute(w, CORE_X, NEAR) for w in w_parts]
    row, col, meta = route(
        expert_ids.reshape(1, toks),
        backup_ids.reshape(1, toks),
        capacity.reshape(1, -1),
        gate.reshape(1, toks),
        held,
    )

    def exchange(rows):
        rows = lax.all_to_all(rows.reshape(owners, BIN, wide), EXPERT, 0, 0, tiled=True)
        return rows.reshape(owners * BIN, wide)

    arrived = [exchange(dispatch(row, tokens, meta, c, held)) for c in chunks]
    at_row, at_col, overs = zip(*[places(a) for a in arrived])
    rows = [regroup(at_row[c], arrived[c]) for c in chunks]
    theirs = [lax.ppermute(rows[c], CORE_X, FAR) for c in chunks]
    over = functools.reduce(jnp.maximum, overs)
    own, sent = [], []
    for c in chunks:
        k = c * CHUNK
        own.append(expert(rows[c], w_in, w_out, k, k, None, F32))
        made = expert(theirs[c], w_in, w_out, k, k, None, F32)
        made = expert(theirs[c], others[c], others[c], 0, CHUNK, made, BF16)
        sent.append(lax.ppermute(made, CORE_X, FAR))
        own[c] = expert(rows[c], others[c], others[c], 0, CHUNK, own[c], F32)
    mixed, flags = None, []
    for c in chunks:
        returned = exchange(back(at_col[c], own[c], sent[c], over))
        mixed, flag = combine(col, returned, c, c == chunks[-1], mixed)
        flags.append(flag)
    around = [[(i, (i + k) % helpers) for i in range(helpers)] for k in range(1, helpers)]
    over = functools.reduce(jnp.maximum, [flags[0]] + [lax.ppermute(flags[0], "helper", a) for a in around])
    return lax.cond(
        over[0, 0] > 0.5,
        lambda ops: general(*ops[1:]),
        lambda ops: ops[0],
        (mixed, tokens, gate, expert_ids[:, 0], backup_ids[:, 0], capacity, w_in, w_out),
    )


def solution(mesh):
    torus = Mesh(
        mesh.devices.reshape(4, 4, 2, mesh.shape["helper"]),
        ("expert_0", "expert_1", "expert_2", "helper"),
    )
    in_specs = (
        P(EXPERT_HELPER, None),
        P(EXPERT_HELPER),
        P(EXPERT_HELPER, None),
        P(EXPERT_HELPER, None),
        P(),
        P(EXPERT, None, "helper"),
        P(EXPERT, "helper", None),
    )
    out_specs = P(EXPERT_HELPER, None)
    return jax.shard_map(
        on_device, mesh=torus, in_specs=in_specs, out_specs=out_specs, check_vma=False
    )
```

```python
import functools

import jax
import jax.numpy as jnp
from jax import lax
from jax.experimental import pallas as pl
from jax.experimental.pallas import tpu as pltpu
from jax.sharding import Mesh
from jax.sharding import PartitionSpec as P

EXPERT = ("expert_0", "expert_1", "expert_2")
EXPERT_HELPER = ("expert_0", "expert_1", "expert_2", "helper")
CHUNK = 2
BIN = 40
LIST = 960
REACH = 576
CORE_X = ("expert_2", "helper")
NEAR = [(0, 1), (1, 0), (2, 3), (3, 2), (5, 6), (6, 5), (7, 4), (4, 7)]
FAR = [(1, 2), (2, 1), (3, 0), (0, 3), (4, 5), (5, 4), (6, 7), (7, 6)]
F32 = jnp.float32
BF16 = jnp.bfloat16
VMEM_LIMIT = 24 * 1024 * 1024


def dot(a, b):
    return jnp.dot(a, b, preferred_element_type=F32)


def dot_nt(a, b):
    return lax.dot_general(a, b, (((1,), (1,)), ((), ())), preferred_element_type=F32)


def iota(shape, dim):
    return lax.broadcasted_iota(jnp.int32, shape, dim)


def ones_where(cond):
    return jnp.where(cond, 1.0, 0.0).astype(BF16)


def params():
    return pltpu.CompilerParams(vmem_limit_bytes=VMEM_LIMIT)


def cost(flops, read):
    return pl.CostEstimate(flops=flops // 8, bytes_accessed=read // 8, transcendentals=0)


def route_kernel(held, first_ref, backup_ref, cap_ref, gate_ref, row_ref, col_ref, meta_ref):
    count = cap_ref.shape[1]
    toks = first_ref.shape[1]
    chunks = held // CHUNK
    ids = iota((count, toks), 0)
    first = first_ref[...]
    backup = backup_ref[...]
    one = jnp.where(ids == first, 1.0, 0.0)
    two = jnp.where(ids == backup, 1.0, 0.0)
    earlier = ones_where(iota((toks, toks), 0) < iota((toks, toks), 1))
    rank = jnp.sum(dot(one.astype(BF16), earlier) * one, axis=0, keepdims=True)
    cap = jnp.broadcast_to(cap_ref[...].astype(F32), (8, count)).astype(BF16)
    limit = dot(cap, one.astype(BF16))[0:1]
    kept = jnp.where(rank < limit, 1.0, 0.0)
    spill = two * (1.0 - kept)
    spill_rank = jnp.sum(dot(spill.astype(BF16), earlier) * spill, axis=0, keepdims=True)
    mine = one * kept
    n_kept = jnp.sum(mine, axis=1, keepdims=True)
    final = mine + spill
    n_all = jnp.sum(final, axis=1, keepdims=True)
    e0, e1 = iota((count, count), 0), iota((count, count), 1)
    wide = jnp.broadcast_to(n_all, (count, count)).astype(BF16)
    start = dot(ones_where((e1 < e0) & (e1 // CHUNK == e0 // CHUNK)), wide)
    fullest = jnp.max(dot(ones_where(e1 // CHUNK == e0 // CHUNK), wide))
    over = jnp.where(fullest > BIN - 1, 1.0, 0.0)
    for c in range(chunks):
        here = e0 % held // CHUNK == c
        value = jnp.where(e1 == e0 % CHUNK, n_all, jnp.where(e1 == CHUNK, over, 0.0))
        meta_ref[c] = jnp.where(here, value, 0.0).astype(BF16)
    place = jnp.sum(final * start[:, 0:1] + spill * n_kept, axis=0, keepdims=True)
    place = place + jnp.where(kept > 0.5, rank, spill_rank)
    chosen = jnp.where(kept > 0.5, first, backup)
    bins = chosen % held // CHUNK * (count // held) + chosen // held
    row = jnp.where(place < BIN - 1, bins.astype(F32) * BIN + place, -1.0)
    row_ref[...] = jnp.broadcast_to(row, (8, toks)).astype(jnp.int32)
    stacked = jnp.where(
        iota((128, toks), 0) == 0,
        jnp.broadcast_to(row, (128, toks)),
        jnp.broadcast_to(gate_ref[...], (128, toks)),
    )
    col_ref[...] = stacked.T


def route(first, backup, capacity, gate, held):
    toks, count = first.shape[1], capacity.shape[1]
    return pl.pallas_call(
        functools.partial(route_kernel, held),
        out_shape=(
            jax.ShapeDtypeStruct((8, toks), jnp.int32),
            jax.ShapeDtypeStruct((toks, 128), F32),
            jax.ShapeDtypeStruct((held // CHUNK, count, count), BF16),
        ),
        compiler_params=params(),
        cost_estimate=cost(4 * toks * toks * count, toks * 512),
        name="route",
    )(first, backup, capacity, gate)


def dispatch_kernel(chunk, held, row_ref, tok_ref, meta_ref, out_ref):
    rows, toks = out_ref.shape[0], tok_ref.shape[0]
    count = meta_ref.shape[1]
    begin = pl.program_id(0) * rows
    at = iota((rows, toks), 0) + (begin + chunk * (count // held) * BIN)
    value = dot(ones_where(at == row_ref[0:1, :]), tok_ref[...])
    out_ref[...] = value.astype(BF16)
    at = iota((rows, count), 0) + begin
    spare = ones_where((at % BIN == BIN - 1) & (at // BIN == iota((rows, count), 1) // held))
    out_ref[:, 0:count] = (value[:, 0:count] + dot(spare, meta_ref[0])).astype(BF16)


def dispatch(row, tokens, meta, chunk, held):
    toks, wide = tokens.shape
    count = meta.shape[1]
    total = count // held * BIN
    block = total // 2
    return pl.pallas_call(
        functools.partial(dispatch_kernel, chunk, held),
        out_shape=jax.ShapeDtypeStruct((total, wide), BF16),
        grid=(total // block,),
        in_specs=[
            pl.BlockSpec((8, toks), lambda i: (0, 0)),
            pl.BlockSpec((toks, wide), lambda i: (0, 0)),
            pl.BlockSpec((1, count, count), lambda i: (chunk, 0, 0)),
        ],
        out_specs=pl.BlockSpec((block, wide), lambda i: (i, 0)),
        compiler_params=params(),
        cost_estimate=cost(2 * total * toks * wide, 2 * (total + toks) * wide),
        name="dispatch",
    )(row, tokens, meta)


def places_kernel(arrived_ref, row_ref, col_ref, over_ref, top_ref):
    total = arrived_ref.shape[0]
    sources = total // BIN
    spare = ones_where(iota((sources, total), 1) == iota((sources, total), 0) * BIN + (BIN - 1))
    meta = dot(spare, arrived_ref[...]).astype(BF16)
    lane = ones_where(iota((8, 128), 0) == iota((8, 128), 1))
    told = dot_nt(lane, meta)
    n = jnp.where(iota((8, sources), 0) < CHUNK, told, 0.0)
    flagged = jnp.max(jnp.where(iota((8, sources), 0) == CHUNK, told, 0.0))
    each = jnp.sum(n, axis=1, keepdims=True)
    full = (jnp.max(each) > REACH - 1) | (jnp.sum(each) > LIST - 1)
    over = jnp.where((flagged > 0.5) | full, 1.0, 0.0)
    over_ref[...] = jnp.broadcast_to(over, (8, 128))
    top = jnp.broadcast_to(each[0:1], (8, 128))
    high = jnp.floor(top * (1.0 / 128.0))
    lane = iota((8, 128), 1)
    top_ref[...] = jnp.where(lane == 0, high, jnp.where(lane == 1, top - high * 128.0, 0.0))
    base = dot(n.astype(BF16), ones_where(iota((sources, sources), 0) < iota((sources, sources), 1)))
    begin = jnp.zeros((8, sources), F32)
    for j in range(CHUNK):
        ahead = iota((8, sources), 0) > j
        begin = begin + jnp.where(ahead, jnp.broadcast_to(n[j : j + 1], (8, sources)), 0.0)
    shift = base - begin + 128.0
    high = jnp.floor(shift * (1.0 / 128.0))
    low = shift - high * 128.0
    spread = ones_where(iota((sources, total), 1) // BIN == iota((sources, total), 0))
    place = dot(high.astype(BF16), spread) * 128.0 + dot(low.astype(BF16), spread) - 128.0
    begin = dot(begin.astype(BF16), spread)
    end = begin + dot(n.astype(BF16), spread)
    r = (iota((8, total), 1) % BIN).astype(F32)
    place = place + r
    inside = (r >= begin) & (r < end) & (place < REACH - 1) & (r < BIN - 1)
    place = jnp.where(iota((8, total), 0) == 0, place, LIST - 2.0 - place)
    index = jnp.where(inside, place + 1.0, 0.0)
    index = jnp.sum(index, axis=0, keepdims=True) - 1.0
    row_ref[...] = jnp.broadcast_to(index, (8, total)).astype(jnp.int32)
    col_ref[...] = jnp.broadcast_to(index, (128, total)).T


def places(arrived):
    total = arrived.shape[0]
    return pl.pallas_call(
        places_kernel,
        out_shape=(
            jax.ShapeDtypeStruct((8, total), jnp.int32),
            jax.ShapeDtypeStruct((total, 128), F32),
            jax.ShapeDtypeStruct((8, 128), F32),
            jax.ShapeDtypeStruct((8, 128), F32),
        ),
        grid=(1,),
        in_specs=[pl.BlockSpec((total, 128), lambda i: (0, 0))],
        out_specs=(
            pl.BlockSpec((8, total), lambda i: (0, 0)),
            pl.BlockSpec((total, 128), lambda i: (0, 0)),
            pl.BlockSpec((8, 128), lambda i: (0, 0)),
            pl.BlockSpec((8, 128), lambda i: (0, 0)),
        ),
        compiler_params=params(),
        cost_estimate=cost(1 << 25, 1 << 19),
        name="places",
    )(arrived)


def regroup_kernel(index_ref, rows_ref, top_ref, out_ref):
    count, many = out_ref.shape[0], rows_ref.shape[0]
    begin = pl.program_id(0) * count
    here = iota((count, many), 0) + begin
    value = dot(ones_where(here == index_ref[0:1, :]), rows_ref[...])
    out_ref[...] = value.astype(BF16)
    spare = jnp.where(iota((count, 128), 0) + begin == LIST - 1, top_ref[0:1, :], 0.0)
    out_ref[:, 0:128] = (value[:, 0:128] + spare).astype(BF16)


def regroup(index, rows, top):
    many, wide = rows.shape
    block = LIST // 2
    return pl.pallas_call(
        regroup_kernel,
        out_shape=jax.ShapeDtypeStruct((LIST, wide), BF16),
        grid=(LIST // block,),
        in_specs=[
            pl.BlockSpec((8, many), lambda i: (0, 0)),
            pl.BlockSpec((many, wide), lambda i: (0, 0)),
            pl.BlockSpec((8, 128), lambda i: (0, 0)),
        ],
        out_specs=pl.BlockSpec((block, wide), lambda i: (i, 0)),
        compiler_params=params(),
        cost_estimate=cost(2 * LIST * many * wide, 2 * (LIST + many) * wide),
        name="regroup",
    )(index, rows, top)


def weights_kernel(first, in_ref, out_ref, both_ref, sems):
    copies = [
        pltpu.make_async_copy(ref.at[first + i], both_ref.at[k * CHUNK + i], sems.at[k * CHUNK + i])
        for k, ref in enumerate((in_ref, out_ref))
        for i in range(CHUNK)
    ]
    for copy in copies:
        copy.start()
    for copy in copies:
        copy.wait()


def weights(w_in, w_out, first):
    _, wide, hid = w_in.shape
    return pl.pallas_call(
        functools.partial(weights_kernel, first),
        out_shape=jax.ShapeDtypeStruct((2 * CHUNK, wide, hid), w_in.dtype),
        in_specs=[pl.BlockSpec(memory_space=pl.ANY)] * 2,
        out_specs=pl.BlockSpec(memory_space=pl.ANY),
        scratch_shapes=[pltpu.SemaphoreType.DMA((2 * CHUNK,))],
        compiler_params=params(),
        cost_estimate=cost(1, 8 * CHUNK * wide * hid),
        name="weights",
    )(w_in, w_out)


def expert_kernel(rows_ref, in0_ref, out0_ref, in1_ref, out1_ref, part_ref, total_ref):
    step = pl.program_id(0)
    spare = rows_ref[LIST - 16 : LIST, 0:128].astype(F32)
    lane = iota((16, 128), 1)
    scale = jnp.where(lane == 0, 128.0, jnp.where(lane == 1, 1.0, 0.0))
    scale = jnp.where(iota((16, 128), 0) == 15, scale, 0.0)
    top = jnp.sum(spare * scale).astype(jnp.int32)

    def term(begin, in_ref, out_ref):
        at = iota((REACH, 1), 0) + begin
        mine = at < top if begin == 0 else at >= top
        rows = jnp.where(mine, rows_ref[begin : begin + REACH, :], jnp.zeros((), BF16))
        hidden = jnp.maximum(dot(rows, in_ref[0]), 0.0).astype(BF16)
        return dot(hidden, out_ref[0])

    @pl.when(step == 0)
    def _():
        total_ref[REACH:LIST, :] = jnp.zeros((LIST - REACH, total_ref.shape[1]), F32)
        total_ref[0:REACH, :] = term(0, in0_ref, out0_ref)

    @pl.when(step == 1)
    def _():
        total_ref[LIST - REACH : LIST, :] += term(LIST - REACH, in0_ref, out0_ref)

    @pl.when(step == 2)
    def _():
        total_ref[0:REACH, :] += term(0, in1_ref, out1_ref)

    @pl.when(step == 3)
    def _():
        total_ref[LIST - REACH : LIST, :] += term(LIST - REACH, in1_ref, out1_ref)
        part_ref[...] = total_ref[...].astype(part_ref.dtype)


def expert(rows, w_in, w_out, first, other, dtype):
    wide, hid = w_in.shape[1], w_in.shape[2]
    own, theirs = lambda i: jnp.minimum(i, CHUNK - 1), lambda i: jnp.maximum(i - CHUNK, 0)
    whole = pl.BlockSpec((LIST, wide), lambda i: (0, 0))
    return pl.pallas_call(
        expert_kernel,
        out_shape=jax.ShapeDtypeStruct((LIST, wide), dtype),
        grid=(2 * CHUNK,),
        in_specs=[
            whole,
            pl.BlockSpec((1, wide, hid), lambda i: (first + own(i), 0, 0)),
            pl.BlockSpec((1, hid, wide), lambda i: (first + own(i), 0, 0)),
            pl.BlockSpec((1, wide, hid), lambda i: (theirs(i), 0, 0)),
            pl.BlockSpec((1, hid, wide), lambda i: (CHUNK + theirs(i), 0, 0)),
        ],
        out_specs=whole,
        scratch_shapes=[pltpu.VMEM((LIST, wide), F32)],
        compiler_params=pltpu.CompilerParams(vmem_limit_bytes=32 * 1024 * 1024),
        cost_estimate=cost(16 * REACH * wide * hid, 8 * CHUNK * wide * hid + 6 * LIST * wide),
        name="expert",
    )(rows, w_in, w_out, other, other)


def back_kernel(col_ref, own_ref, sent_ref, over_ref, out_ref):
    rows, many = out_ref.shape[0], own_ref.shape[0]
    value = (own_ref[...] + sent_ref[...].astype(F32)).astype(BF16)
    col = col_ref[:, 0:1].astype(jnp.int32)
    result = dot(ones_where(col == iota((rows, many), 1)), value)
    out_ref[...] = result.astype(BF16)
    at = iota((rows, 128), 0) + pl.program_id(0) * rows
    flag = jnp.where(at % BIN == BIN - 1, over_ref[0:1, :], 0.0)
    out_ref[:, 0:128] = (result[:, 0:128] + flag).astype(BF16)


def back(col, own, sent, over):
    total, (many, wide) = col.shape[0], own.shape
    block = total // 2
    whole = pl.BlockSpec((many, wide), lambda i: (0, 0))
    return pl.pallas_call(
        back_kernel,
        out_shape=jax.ShapeDtypeStruct((total, wide), BF16),
        grid=(total // block,),
        in_specs=[
            pl.BlockSpec((block, 128), lambda i: (i, 0)),
            whole,
            whole,
            pl.BlockSpec((8, 128), lambda i: (0, 0)),
        ],
        out_specs=pl.BlockSpec((block, wide), lambda i: (i, 0)),
        compiler_params=params(),
        cost_estimate=cost(2 * total * many * wide, 2 * total * wide + 6 * many * wide),
        name="back",
    )(col, own, sent, over)


def combine_kernel(chunk, last, col_ref, returned_ref, *refs):
    rows, many = refs[-2].shape[0], returned_ref.shape[0]
    col = col_ref[:, 0:1].astype(jnp.int32)
    total = dot(ones_where(col - chunk * many == iota((rows, many), 1)), returned_ref[...])
    if chunk > 0:
        total = total + refs[0][...].astype(F32)
    if last:
        total = total * col_ref[:, 1:2]
    refs[-2][...] = total.astype(BF16)
    spare = iota((many, 128), 0) % BIN == BIN - 1
    over = jnp.max(jnp.where(spare, returned_ref[:, 0:128].astype(F32), 0.0))
    refs[-1][...] = jnp.broadcast_to(over, (8, 128))


def combine(col, returned, chunk, last, so_far):
    toks, (many, wide) = col.shape[0], returned.shape
    block = toks // 2
    extra = [] if so_far is None else [so_far]
    return pl.pallas_call(
        functools.partial(combine_kernel, chunk, last),
        out_shape=(
            jax.ShapeDtypeStruct((toks, wide), BF16),
            jax.ShapeDtypeStruct((8, 128), F32),
        ),
        grid=(toks // block,),
        in_specs=[
            pl.BlockSpec((block, 128), lambda i: (i, 0)),
            pl.BlockSpec((many, wide), lambda i: (0, 0)),
        ]
        + [pl.BlockSpec((block, wide), lambda i: (i, 0))] * len(extra),
        out_specs=(
            pl.BlockSpec((block, wide), lambda i: (i, 0)),
            pl.BlockSpec((8, 128), lambda i: (0, 0)),
        ),
        compiler_params=params(),
        cost_estimate=cost(2 * toks * many * wide, 2 * (many + 2 * toks) * wide),
        name="combine",
    )(col, returned, *extra)


def assign(first, backup, capacity, count, slot):
    columns = jnp.arange(count, dtype=jnp.int32)
    where = jnp.arange(first.shape[0], dtype=jnp.int32)
    earlier = ones_where(where[None, :] < where[:, None])
    onehot = (first[:, None] == columns[None, :]).astype(F32)
    rank = jnp.sum(dot(earlier, onehot.astype(BF16)) * onehot, axis=1)
    limit = jnp.sum(onehot * capacity[None, :].astype(F32), axis=1)
    kept = rank < limit
    spill = jnp.where((backup[:, None] == columns[None, :]) & ~kept[:, None], 1.0, 0.0)
    spill_rank = jnp.sum(dot(earlier, spill.astype(BF16)) * spill, axis=1)
    final = jnp.where(kept, first, backup)
    slots = jnp.where(kept, rank, slot + spill_rank).astype(jnp.int32)
    return slots, final


def general(tokens, gate, first, backup, capacity, w_in, w_out):
    held = w_in.shape[0]
    owners = lax.axis_size(EXPERT)
    helpers = lax.axis_size("helper")
    experts = held * owners
    slot = max(6, 3 * tokens.shape[0] // (2 * experts))
    slots, final = assign(first, backup, capacity, experts, slot)
    wide = tokens.shape[1]
    buffer = jnp.zeros((experts, 2 * slot, wide), BF16).at[final, slots].set(tokens)
    buffer = buffer.reshape(owners, held * 2 * slot, wide)
    arrived = lax.all_to_all(buffer, EXPERT, 0, 0, tiled=True)
    arrived = arrived.reshape(owners, held, 2 * slot, wide)
    rows = [arrived[:, e].reshape(owners * 2 * slot, wide) for e in range(held)]
    totals = [jnp.zeros(r.shape, F32) for r in rows]
    for k in range(helpers):
        turn = [(i, (i + k) % helpers) for i in range(helpers)]
        some_in = lax.ppermute(w_in, "helper", turn) if k else w_in
        some_out = lax.ppermute(w_out, "helper", turn) if k else w_out
        for e in range(held):
            hidden = jnp.maximum(dot(rows[e], some_in[e]), 0.0).astype(BF16)
            totals[e] = totals[e] + dot(hidden, some_out[e]).astype(BF16).astype(F32)
    outputs = [t.astype(BF16).reshape(owners, 2 * slot, wide) for t in totals]
    result = jnp.stack(outputs, axis=1).reshape(owners, held * 2 * slot, wide)
    returned = lax.all_to_all(result, EXPERT, 0, 0, tiled=True)
    picked = returned.reshape(experts, 2 * slot, wide)[final, slots]
    return (gate[:, None] * picked.astype(F32)).astype(BF16)


def after(*values):
    return lax.optimization_barrier(values)


def on_device(tokens, gate, expert_ids, backup_ids, capacity, w_in, w_out):
    held = w_in.shape[0]
    owners = lax.axis_size(EXPERT)
    helpers = lax.axis_size("helper")
    toks, wide = tokens.shape
    chunks = range(held // CHUNK)
    w_parts = [weights(w_in, w_out, c * CHUNK) for c in chunks]
    others = [lax.ppermute(w, CORE_X, NEAR) for w in w_parts]
    row, col, meta = route(
        expert_ids.reshape(1, toks),
        backup_ids.reshape(1, toks),
        capacity.reshape(1, -1),
        gate.reshape(1, toks),
        held,
    )

    def exchange(rows):
        rows = lax.all_to_all(rows.reshape(owners, BIN, wide), EXPERT, 0, 0, tiled=True)
        return rows.reshape(owners * BIN, wide)

    arrived = [exchange(dispatch(row, tokens, meta, c, held)) for c in chunks]
    at_row, at_col, overs, tops = zip(*[places(a) for a in arrived])
    rows = [regroup(at_row[c], arrived[c], tops[c]) for c in chunks]
    theirs = [lax.ppermute(rows[c], CORE_X, FAR) for c in chunks]
    over = functools.reduce(jnp.maximum, overs)
    own, sent = [], []
    for c in chunks:
        k = c * CHUNK
        args = (w_in, w_out, k, others[c])
        sent.append(lax.ppermute(expert(theirs[c], *args, BF16), CORE_X, FAR))
        own.append(expert(rows[c], *args, F32))
    mixed, flags = None, []
    for c in chunks:
        returned = exchange(back(at_col[c], own[c], sent[c], over))
        mixed, flag = combine(col, returned, c, c == chunks[-1], mixed)
        flags.append(flag)
    around = [[(i, (i + k) % helpers) for i in range(helpers)] for k in range(1, helpers)]
    over = functools.reduce(jnp.maximum, [flags[0]] + [lax.ppermute(flags[0], "helper", a) for a in around])
    return lax.cond(
        over[0, 0] > 0.5,
        lambda ops: general(*ops[1:]),
        lambda ops: ops[0],
        (mixed, tokens, gate, expert_ids[:, 0], backup_ids[:, 0], capacity, w_in, w_out),
    )


def solution(mesh):
    torus = Mesh(
        mesh.devices.reshape(4, 4, 2, mesh.shape["helper"]),
        ("expert_0", "expert_1", "expert_2", "helper"),
    )
    in_specs = (
        P(EXPERT_HELPER, None),
        P(EXPERT_HELPER),
        P(EXPERT_HELPER, None),
        P(EXPERT_HELPER, None),
        P(),
        P(EXPERT, None, "helper"),
        P(EXPERT, "helper", None),
    )
    out_specs = P(EXPERT_HELPER, None)
    return jax.shard_map(
        on_device, mesh=torus, in_specs=in_specs, out_specs=out_specs, check_vma=False
    )
```

```python
import functools

import jax
import jax.numpy as jnp
from jax import lax
from jax.experimental import pallas as pl
from jax.experimental.pallas import tpu as pltpu
from jax.sharding import Mesh
from jax.sharding import PartitionSpec as P

EXPERT = ("expert_0", "expert_1", "expert_2")
EXPERT_HELPER = ("expert_0", "expert_1", "expert_2", "helper")
CHUNK = 2
BIN = 40
LIST = 960
REACH = 576
WHOLE = ((0, LIST),)
PARTS = (WHOLE, ((0, 480), (480, 480)))
CORE_X = ("expert_2", "helper")
NEAR = [(0, 1), (1, 0), (2, 3), (3, 2), (5, 6), (6, 5), (7, 4), (4, 7)]
FAR = [(1, 2), (2, 1), (3, 0), (0, 3), (4, 5), (5, 4), (6, 7), (7, 6)]
F32 = jnp.float32
BF16 = jnp.bfloat16
VMEM_LIMIT = 24 * 1024 * 1024


def dot(a, b):
    return jnp.dot(a, b, preferred_element_type=F32)


def dot_nt(a, b):
    return lax.dot_general(a, b, (((1,), (1,)), ((), ())), preferred_element_type=F32)


def iota(shape, dim):
    return lax.broadcasted_iota(jnp.int32, shape, dim)


def ones_where(cond):
    return jnp.where(cond, 1.0, 0.0).astype(BF16)


def params():
    return pltpu.CompilerParams(vmem_limit_bytes=VMEM_LIMIT)


def cost(flops, read):
    return pl.CostEstimate(flops=flops, bytes_accessed=read, transcendentals=0)


def route_kernel(held, first_ref, backup_ref, cap_ref, gate_ref, row_ref, col_ref, meta_ref):
    count = cap_ref.shape[1]
    toks = first_ref.shape[1]
    chunks = held // CHUNK
    ids = iota((count, toks), 0)
    first = first_ref[...]
    backup = backup_ref[...]
    one = jnp.where(ids == first, 1.0, 0.0)
    two = jnp.where(ids == backup, 1.0, 0.0)
    earlier = ones_where(iota((toks, toks), 0) < iota((toks, toks), 1))
    rank = jnp.sum(dot(one.astype(BF16), earlier) * one, axis=0, keepdims=True)
    cap = jnp.broadcast_to(cap_ref[...].astype(F32), (8, count)).astype(BF16)
    limit = dot(cap, one.astype(BF16))[0:1]
    kept = jnp.where(rank < limit, 1.0, 0.0)
    spill = two * (1.0 - kept)
    spill_rank = jnp.sum(dot(spill.astype(BF16), earlier) * spill, axis=0, keepdims=True)
    mine = one * kept
    n_kept = jnp.sum(mine, axis=1, keepdims=True)
    final = mine + spill
    n_all = jnp.sum(final, axis=1, keepdims=True)
    e0, e1 = iota((count, count), 0), iota((count, count), 1)
    wide = jnp.broadcast_to(n_all, (count, count)).astype(BF16)
    start = dot(ones_where((e1 < e0) & (e1 // CHUNK == e0 // CHUNK)), wide)
    fullest = jnp.max(dot(ones_where(e1 // CHUNK == e0 // CHUNK), wide))
    over = jnp.where(fullest > BIN - 1, 1.0, 0.0)
    for c in range(chunks):
        here = e0 % held // CHUNK == c
        value = jnp.where(e1 == e0 % CHUNK, n_all, jnp.where(e1 == CHUNK, over, 0.0))
        meta_ref[c] = jnp.where(here, value, 0.0).astype(BF16)
    place = jnp.sum(final * start[:, 0:1] + spill * n_kept, axis=0, keepdims=True)
    place = place + jnp.where(kept > 0.5, rank, spill_rank)
    chosen = jnp.where(kept > 0.5, first, backup)
    bins = chosen % held // CHUNK * (count // held) + chosen // held
    row = jnp.where(place < BIN - 1, bins.astype(F32) * BIN + place, -1.0)
    row_ref[...] = jnp.broadcast_to(row, (8, toks)).astype(jnp.int32)
    stacked = jnp.where(
        iota((128, toks), 0) == 0,
        jnp.broadcast_to(row, (128, toks)),
        jnp.broadcast_to(gate_ref[...], (128, toks)),
    )
    col_ref[...] = stacked.T


def route(first, backup, capacity, gate, held):
    toks, count = first.shape[1], capacity.shape[1]
    return pl.pallas_call(
        functools.partial(route_kernel, held),
        out_shape=(
            jax.ShapeDtypeStruct((8, toks), jnp.int32),
            jax.ShapeDtypeStruct((toks, 128), F32),
            jax.ShapeDtypeStruct((held // CHUNK, count, count), BF16),
        ),
        compiler_params=params(),
        cost_estimate=cost(4 * toks * toks * count, toks * 512),
        name="route",
    )(first, backup, capacity, gate)


def dispatch_kernel(chunk, held, row_ref, tok_ref, meta_ref, out_ref):
    rows, toks = out_ref.shape[0], tok_ref.shape[0]
    count = meta_ref.shape[1]
    begin = pl.program_id(0) * rows
    at = iota((rows, toks), 0) + (begin + chunk * (count // held) * BIN)
    value = dot(ones_where(at == row_ref[0:1, :]), tok_ref[...])
    out_ref[...] = value.astype(BF16)
    at = iota((rows, count), 0) + begin
    spare = ones_where((at % BIN == BIN - 1) & (at // BIN == iota((rows, count), 1) // held))
    out_ref[:, 0:count] = (value[:, 0:count] + dot(spare, meta_ref[0])).astype(BF16)


def dispatch(row, tokens, meta, chunk, held):
    toks, wide = tokens.shape
    count = meta.shape[1]
    total = count // held * BIN
    block = total // 2
    return pl.pallas_call(
        functools.partial(dispatch_kernel, chunk, held),
        out_shape=jax.ShapeDtypeStruct((total, wide), BF16),
        grid=(total // block,),
        in_specs=[
            pl.BlockSpec((8, toks), lambda i: (0, 0)),
            pl.BlockSpec((toks, wide), lambda i: (0, 0)),
            pl.BlockSpec((1, count, count), lambda i: (chunk, 0, 0)),
        ],
        out_specs=pl.BlockSpec((block, wide), lambda i: (i, 0)),
        compiler_params=params(),
        cost_estimate=cost(2 * total * toks * wide, 2 * (total + toks) * wide),
        name="dispatch",
    )(row, tokens, meta)


def places_kernel(arrived_ref, row_ref, col_ref, over_ref, top_ref):
    total = arrived_ref.shape[0]
    sources = total // BIN
    spare = ones_where(iota((sources, total), 1) == iota((sources, total), 0) * BIN + (BIN - 1))
    meta = dot(spare, arrived_ref[...]).astype(BF16)
    lane = ones_where(iota((8, 128), 0) == iota((8, 128), 1))
    told = dot_nt(lane, meta)
    n = jnp.where(iota((8, sources), 0) < CHUNK, told, 0.0)
    flagged = jnp.max(jnp.where(iota((8, sources), 0) == CHUNK, told, 0.0))
    each = jnp.sum(n, axis=1, keepdims=True)
    full = (jnp.max(each) > REACH - 1) | (jnp.sum(each) > LIST - 2)
    over = jnp.where((flagged > 0.5) | full, 1.0, 0.0)
    over_ref[...] = jnp.broadcast_to(over, (8, 128))
    top = jnp.broadcast_to(each[0:1] + 1.0, (8, 128))
    high = jnp.floor(top * (1.0 / 128.0))
    lane = iota((8, 128), 1)
    top_ref[...] = jnp.where(lane == 0, high, jnp.where(lane == 1, top - high * 128.0, 0.0))
    base = dot(n.astype(BF16), ones_where(iota((sources, sources), 0) < iota((sources, sources), 1)))
    begin = jnp.zeros((8, sources), F32)
    for j in range(CHUNK):
        ahead = iota((8, sources), 0) > j
        begin = begin + jnp.where(ahead, jnp.broadcast_to(n[j : j + 1], (8, sources)), 0.0)
    shift = base - begin + 128.0
    high = jnp.floor(shift * (1.0 / 128.0))
    low = shift - high * 128.0
    spread = ones_where(iota((sources, total), 1) // BIN == iota((sources, total), 0))
    place = dot(high.astype(BF16), spread) * 128.0 + dot(low.astype(BF16), spread) - 128.0
    begin = dot(begin.astype(BF16), spread)
    end = begin + dot(n.astype(BF16), spread)
    r = (iota((8, total), 1) % BIN).astype(F32)
    place = place + r
    inside = (r >= begin) & (r < end) & (place < REACH - 1) & (r < BIN - 1)
    place = jnp.where(iota((8, total), 0) == 0, place + 1.0, LIST - 2.0 - place)
    index = jnp.where(inside, place + 1.0, 0.0)
    index = jnp.sum(index, axis=0, keepdims=True) - 1.0
    row_ref[...] = jnp.broadcast_to(index, (8, total)).astype(jnp.int32)
    col_ref[...] = jnp.broadcast_to(index, (128, total)).T


def places(arrived):
    total = arrived.shape[0]
    return pl.pallas_call(
        places_kernel,
        out_shape=(
            jax.ShapeDtypeStruct((8, total), jnp.int32),
            jax.ShapeDtypeStruct((total, 128), F32),
            jax.ShapeDtypeStruct((8, 128), F32),
            jax.ShapeDtypeStruct((8, 128), F32),
        ),
        grid=(1,),
        in_specs=[pl.BlockSpec((total, 128), lambda i: (0, 0))],
        out_specs=(
            pl.BlockSpec((8, total), lambda i: (0, 0)),
            pl.BlockSpec((total, 128), lambda i: (0, 0)),
            pl.BlockSpec((8, 128), lambda i: (0, 0)),
            pl.BlockSpec((8, 128), lambda i: (0, 0)),
        ),
        compiler_params=params(),
        cost_estimate=cost(1 << 25, 1 << 19),
        name="places",
    )(arrived)


def regroup_kernel(index_ref, rows_ref, top_ref, out_ref):
    count, many = out_ref.shape[0], rows_ref.shape[0]
    begin = pl.program_id(0) * count
    here = iota((count, many), 0) + begin
    value = dot(ones_where(here == index_ref[0:1, :]), rows_ref[...])
    out_ref[...] = value.astype(BF16)
    at = iota((count, 128), 0) + begin
    spare = jnp.where((at == 0) | (at == LIST - 1), top_ref[0:1, :], 0.0)
    out_ref[:, 0:128] = (value[:, 0:128] + spare).astype(BF16)


def regroup(index, rows, top):
    many, wide = rows.shape
    count, block = LIST, LIST // 2
    return pl.pallas_call(
        regroup_kernel,
        out_shape=jax.ShapeDtypeStruct((count, wide), BF16),
        grid=(count // block,),
        in_specs=[
            pl.BlockSpec((8, many), lambda i: (0, 0)),
            pl.BlockSpec((many, wide), lambda i: (0, 0)),
            pl.BlockSpec((8, 128), lambda i: (0, 0)),
        ],
        out_specs=pl.BlockSpec((block, wide), lambda i: (i, 0)),
        compiler_params=params(),
        cost_estimate=cost(2 * count * many * wide, 2 * (count + many) * wide),
        name="regroup",
    )(index, rows, top)


def weights_kernel(first, in_ref, out_ref, both_ref, held_ref, read_sems, write_sems):
    reads, writes = [], []
    for k, ref in enumerate((in_ref, out_ref)):
        for i in range(CHUNK):
            at = k * CHUNK + i
            reads.append(pltpu.make_async_copy(ref.at[first + i], held_ref.at[at], read_sems.at[at]))
            writes.append(pltpu.make_async_copy(held_ref.at[at], both_ref.at[at], write_sems.at[at]))
    for read in reads:
        read.start()
    for read, write in zip(reads, writes):
        read.wait()
        write.start()
    for write in writes:
        write.wait()


def weights(w_in, w_out, first):
    _, wide, hid = w_in.shape
    shape = (2 * CHUNK, wide, hid)
    return pl.pallas_call(
        functools.partial(weights_kernel, first),
        out_shape=jax.ShapeDtypeStruct(shape, w_in.dtype),
        in_specs=[pl.BlockSpec(memory_space=pl.ANY)] * 2,
        out_specs=pl.BlockSpec(memory_space=pl.ANY),
        scratch_shapes=[
            pltpu.VMEM(shape, w_in.dtype),
            pltpu.SemaphoreType.DMA((2 * CHUNK,)),
            pltpu.SemaphoreType.DMA((2 * CHUNK,)),
        ],
        compiler_params=params(),
        cost_estimate=cost(1, 8 * CHUNK * wide * hid),
        name="weights",
    )(w_in, w_out)


def expert_kernel(parts, *refs):
    n = len(parts)
    rows_refs, weight_refs = refs[:n], refs[n : n + 4]
    part_refs, total_refs = refs[-2 * n : -n], refs[-n:]
    step = pl.program_id(0)
    at = 0 if parts[0][0] == 0 else parts[0][1] - 16
    lane, line = iota((16, 128), 1), iota((16, 128), 0)
    scale = jnp.where(lane == 0, 128.0, jnp.where(lane == 1, 1.0, 0.0))
    scale = jnp.where(line == (0 if at == 0 else 15), scale, 0.0)
    top = jnp.sum(rows_refs[0][at : at + 16, 0:128].astype(F32) * scale).astype(jnp.int32)

    def add(upper, begins):
        in0_ref, out0_ref, in1_ref, out1_ref = weight_refs
        reach = (0, REACH) if upper else (LIST - REACH, LIST)
        for (first, count), rows_ref, total_ref in zip(parts, rows_refs, total_refs):
            low, high = max(reach[0] - first, 0), min(reach[1] - first, count)
            if begins and low > 0:
                total_ref[0:low, :] = jnp.zeros((low, total_ref.shape[1]), F32)
            if begins and high < count:
                total_ref[high:count, :] = jnp.zeros((count - high, total_ref.shape[1]), F32)
            place = iota((high - low, 1), 0) + (first + low)
            mine = place < top if upper else place >= top
            rows = jnp.where(mine, rows_ref[low:high, :], jnp.zeros((), BF16))
            term = None
            for in_ref, out_ref in ((in0_ref, out0_ref), (in1_ref, out1_ref)):
                hidden = jnp.maximum(dot(rows, in_ref[0]), 0.0).astype(BF16)
                part = dot(hidden, out_ref[0])
                term = part if term is None else term + part
            total_ref[low:high, :] = term if begins else total_ref[low:high, :] + term

    for k in range(CHUNK):

        @pl.when(step == k)
        def _(k=k):
            add(k == 0, k == 0)
            if k == CHUNK - 1:
                for part_ref, total_ref in zip(part_refs, total_refs):
                    part_ref[...] = total_ref[...].astype(part_ref.dtype)


def expert(rows, parts, w_in, w_out, first, other, dtype, later_than=()):
    wide, hid = w_in.shape[1], w_in.shape[2]
    total = sum(count for _, count in parts)
    wholes = [pl.BlockSpec((count, wide), lambda i: (0, 0)) for _, count in parts]
    taken = [pl.BlockSpec((c, wide), lambda i, f=f, c=c: (f // c, 0)) for f, c in parts]
    made = pl.pallas_call(
        functools.partial(expert_kernel, parts),
        out_shape=[jax.ShapeDtypeStruct((count, wide), dtype) for _, count in parts],
        grid=(CHUNK,),
        in_specs=taken
        + [
            pl.BlockSpec((1, wide, hid), lambda i: (first + i, 0, 0)),
            pl.BlockSpec((1, hid, wide), lambda i: (first + i, 0, 0)),
            pl.BlockSpec((1, wide, hid), lambda i: (i, 0, 0)),
            pl.BlockSpec((1, hid, wide), lambda i: (CHUNK + i, 0, 0)),
        ]
        + [pl.BlockSpec(memory_space=pl.ANY)] * len(later_than),
        out_specs=wholes,
        scratch_shapes=[pltpu.VMEM((count, wide), F32) for _, count in parts],
        compiler_params=pltpu.CompilerParams(vmem_limit_bytes=32 * 1024 * 1024),
        cost_estimate=cost(8 * total * wide * hid, 8 * CHUNK * wide * hid + 6 * total * wide),
        name="expert",
    )(*[rows] * len(parts), w_in, w_out, other, other, *later_than)
    return list(made)


def back_kernel(parts, col_ref, over_ref, *refs):
    n, out_ref = len(parts), refs[-1]
    rows = out_ref.shape[0]
    col = col_ref[:, 0:1].astype(jnp.int32)
    result = None
    for i, (first, count) in enumerate(parts):
        value = (refs[i][...] + refs[n + i][...].astype(F32)).astype(BF16)
        part = dot(ones_where(col - first == iota((rows, count), 1)), value)
        result = part if result is None else result + part
    out_ref[...] = result.astype(BF16)
    at = iota((rows, 128), 0) + pl.program_id(0) * rows
    flag = jnp.where(at % BIN == BIN - 1, over_ref[0:1, :], 0.0)
    out_ref[:, 0:128] = (result[:, 0:128] + flag).astype(BF16)


def back(col, own, sent, over, parts):
    total, wide = col.shape[0], own.shape[1]
    block = total // 2
    wholes = [pl.BlockSpec((count, wide), lambda i: (0, 0)) for _, count in parts]
    taken = [pl.BlockSpec((c, wide), lambda i, f=f, c=c: (f // c, 0)) for f, c in parts]
    return pl.pallas_call(
        functools.partial(back_kernel, parts),
        out_shape=jax.ShapeDtypeStruct((total, wide), BF16),
        grid=(total // block,),
        in_specs=[
            pl.BlockSpec((block, 128), lambda i: (i, 0)),
            pl.BlockSpec((8, 128), lambda i: (0, 0)),
        ]
        + taken
        + wholes,
        out_specs=pl.BlockSpec((block, wide), lambda i: (i, 0)),
        compiler_params=params(),
        cost_estimate=cost(2 * total * LIST * wide, 2 * total * wide + 6 * LIST * wide),
        name="back",
    )(col, over, *[own] * len(parts), *sent)


def combine_kernel(chunk, last, col_ref, returned_ref, *refs):
    rows, many = refs[-2].shape[0], returned_ref.shape[0]
    col = col_ref[:, 0:1].astype(jnp.int32)
    total = dot(ones_where(col - chunk * many == iota((rows, many), 1)), returned_ref[...])
    if chunk > 0:
        total = total + refs[0][...].astype(F32)
    if last:
        total = total * col_ref[:, 1:2]
    refs[-2][...] = total.astype(BF16)
    spare = iota((many, 128), 0) % BIN == BIN - 1
    over = jnp.max(jnp.where(spare, returned_ref[:, 0:128].astype(F32), 0.0))
    refs[-1][...] = jnp.broadcast_to(over, (8, 128))


def combine(col, returned, chunk, last, so_far):
    toks, (many, wide) = col.shape[0], returned.shape
    block = toks // 2
    extra = [] if so_far is None else [so_far]
    return pl.pallas_call(
        functools.partial(combine_kernel, chunk, last),
        out_shape=(
            jax.ShapeDtypeStruct((toks, wide), BF16),
            jax.ShapeDtypeStruct((8, 128), F32),
        ),
        grid=(toks // block,),
        in_specs=[
            pl.BlockSpec((block, 128), lambda i: (i, 0)),
            pl.BlockSpec((many, wide), lambda i: (0, 0)),
        ]
        + [pl.BlockSpec((block, wide), lambda i: (i, 0))] * len(extra),
        out_specs=(
            pl.BlockSpec((block, wide), lambda i: (i, 0)),
            pl.BlockSpec((8, 128), lambda i: (0, 0)),
        ),
        compiler_params=params(),
        cost_estimate=cost(2 * toks * many * wide, 2 * (many + 2 * toks) * wide),
        name="combine",
    )(col, returned, *extra)


def assign(first, backup, capacity, count, slot):
    columns = jnp.arange(count, dtype=jnp.int32)
    where = jnp.arange(first.shape[0], dtype=jnp.int32)
    earlier = ones_where(where[None, :] < where[:, None])
    onehot = (first[:, None] == columns[None, :]).astype(F32)
    rank = jnp.sum(dot(earlier, onehot.astype(BF16)) * onehot, axis=1)
    limit = jnp.sum(onehot * capacity[None, :].astype(F32), axis=1)
    kept = rank < limit
    spill = jnp.where((backup[:, None] == columns[None, :]) & ~kept[:, None], 1.0, 0.0)
    spill_rank = jnp.sum(dot(earlier, spill.astype(BF16)) * spill, axis=1)
    final = jnp.where(kept, first, backup)
    slots = jnp.where(kept, rank, slot + spill_rank).astype(jnp.int32)
    return slots, final


def general(tokens, gate, first, backup, capacity, w_in, w_out):
    held = w_in.shape[0]
    owners = lax.axis_size(EXPERT)
    helpers = lax.axis_size("helper")
    experts = held * owners
    slot = max(6, 3 * tokens.shape[0] // (2 * experts))
    slots, final = assign(first, backup, capacity, experts, slot)
    wide = tokens.shape[1]
    buffer = jnp.zeros((experts, 2 * slot, wide), BF16).at[final, slots].set(tokens)
    buffer = buffer.reshape(owners, held * 2 * slot, wide)
    arrived = lax.all_to_all(buffer, EXPERT, 0, 0, tiled=True)
    arrived = arrived.reshape(owners, held, 2 * slot, wide)
    rows = [arrived[:, e].reshape(owners * 2 * slot, wide) for e in range(held)]
    totals = [jnp.zeros(r.shape, F32) for r in rows]
    for k in range(helpers):
        turn = [(i, (i + k) % helpers) for i in range(helpers)]
        some_in = lax.ppermute(w_in, "helper", turn) if k else w_in
        some_out = lax.ppermute(w_out, "helper", turn) if k else w_out
        for e in range(held):
            hidden = jnp.maximum(dot(rows[e], some_in[e]), 0.0).astype(BF16)
            totals[e] = totals[e] + dot(hidden, some_out[e]).astype(BF16).astype(F32)
    outputs = [t.astype(BF16).reshape(owners, 2 * slot, wide) for t in totals]
    result = jnp.stack(outputs, axis=1).reshape(owners, held * 2 * slot, wide)
    returned = lax.all_to_all(result, EXPERT, 0, 0, tiled=True)
    picked = returned.reshape(experts, 2 * slot, wide)[final, slots]
    return (gate[:, None] * picked.astype(F32)).astype(BF16)


def after(*values):
    return lax.optimization_barrier(values)


def on_device(tokens, gate, expert_ids, backup_ids, capacity, w_in, w_out):
    held = w_in.shape[0]
    owners = lax.axis_size(EXPERT)
    helpers = lax.axis_size("helper")
    toks, wide = tokens.shape
    chunks = range(held // CHUNK)
    w_parts = [weights(w_in, w_out, c * CHUNK) for c in chunks]
    others = [lax.ppermute(w, CORE_X, NEAR) for w in w_parts]
    row, col, meta = route(
        expert_ids.reshape(1, toks),
        backup_ids.reshape(1, toks),
        capacity.reshape(1, -1),
        gate.reshape(1, toks),
        held,
    )

    def exchange(rows):
        rows = lax.all_to_all(rows.reshape(owners, BIN, wide), EXPERT, 0, 0, tiled=True)
        return rows.reshape(owners * BIN, wide)

    arrived = [exchange(dispatch(row, tokens, meta, c, held)) for c in chunks]
    at_row, at_col, overs, tops = zip(*[places(a) for a in arrived])
    rows = [regroup(at_row[c], arrived[c], tops[c]) for c in chunks]
    theirs = [lax.ppermute(r, CORE_X, FAR) for r in rows]
    over = functools.reduce(jnp.maximum, overs)
    own, sent = [], []
    for c in chunks:
        k = c * CHUNK
        args = (w_in, w_out, k, others[c])
        made = [expert(theirs[c], [p], *args, BF16)[0] for p in PARTS[c]]
        sent.append([lax.ppermute(m, CORE_X, FAR) for m in made])
        ahead = [rows[c + 1]] if c < chunks[-1] else []
        own.append(expert(rows[c], WHOLE, *args, F32, ahead)[0])
    mixed, flags = None, []
    for c in chunks:
        returned = exchange(back(at_col[c], own[c], sent[c], over, PARTS[c]))
        mixed, flag = combine(col, returned, c, c == chunks[-1], mixed)
        flags.append(flag)
    around = [[(i, (i + k) % helpers) for i in range(helpers)] for k in range(1, helpers)]
    over = functools.reduce(jnp.maximum, [flags[0]] + [lax.ppermute(flags[0], "helper", a) for a in around])
    again = (tokens, gate, expert_ids[:, 0], backup_ids[:, 0], capacity, w_in, w_out)
    _, mixed = lax.while_loop(
        lambda state: state[0] > 0.5,
        lambda state: (jnp.zeros_like(state[0]), general(*again)),
        (over[0, 0], mixed),
    )
    return mixed


def solution(mesh):
    torus = Mesh(
        mesh.devices.reshape(4, 4, 2, mesh.shape["helper"]),
        ("expert_0", "expert_1", "expert_2", "helper"),
    )
    in_specs = (
        P(EXPERT_HELPER, None),
        P(EXPERT_HELPER),
        P(EXPERT_HELPER, None),
        P(EXPERT_HELPER, None),
        P(),
        P(EXPERT, None, "helper"),
        P(EXPERT, "helper", None),
    )
    out_specs = P(EXPERT_HELPER, None)
    return jax.shard_map(
        on_device, mesh=torus, in_specs=in_specs, out_specs=out_specs, check_vma=False
    )
```

```python
import functools

import jax
import jax.numpy as jnp
from jax import lax
from jax.experimental import pallas as pl
from jax.experimental.pallas import tpu as pltpu
from jax.sharding import Mesh
from jax.sharding import PartitionSpec as P

EXPERT = ("expert_0", "expert_1", "expert_2")
EXPERT_HELPER = ("expert_0", "expert_1", "expert_2", "helper")
CHUNK = 2
BIN = 40
LIST = 960
REACH = 576
PARTS = (((0, 960),), ((0, 480), (480, 480)))
CORE_X = ("expert_2", "helper")
NEAR = [(0, 1), (1, 0), (2, 3), (3, 2), (5, 6), (6, 5), (7, 4), (4, 7)]
FAR = [(1, 2), (2, 1), (3, 0), (0, 3), (4, 5), (5, 4), (6, 7), (7, 6)]
F32 = jnp.float32
BF16 = jnp.bfloat16
VMEM_LIMIT = 24 * 1024 * 1024


def dot(a, b):
    return jnp.dot(a, b, preferred_element_type=F32)


def dot_nt(a, b):
    return lax.dot_general(a, b, (((1,), (1,)), ((), ())), preferred_element_type=F32)


def turned(rows):
    return jnp.concatenate([rows, jnp.zeros((120, rows.shape[1]), F32)], axis=0).T


def iota(shape, dim):
    return lax.broadcasted_iota(jnp.int32, shape, dim)


def ones_where(cond):
    return jnp.where(cond, 1.0, 0.0).astype(BF16)


def params():
    return pltpu.CompilerParams(vmem_limit_bytes=VMEM_LIMIT)


def cost(flops, read):
    return pl.CostEstimate(flops=flops, bytes_accessed=read, transcendentals=0)


def route_kernel(held, first_ref, backup_ref, cap_ref, gate_ref, row_ref, meta_ref):
    count = cap_ref.shape[1]
    toks = first_ref.shape[1]
    chunks = held // CHUNK
    ids = iota((count, toks), 0)
    first = first_ref[...]
    backup = backup_ref[...]
    one = jnp.where(ids == first, 1.0, 0.0)
    two = jnp.where(ids == backup, 1.0, 0.0)
    earlier = ones_where(iota((toks, toks), 0) < iota((toks, toks), 1))
    rank = jnp.sum(dot(one.astype(BF16), earlier) * one, axis=0, keepdims=True)
    cap = jnp.broadcast_to(cap_ref[...].astype(F32), (8, count)).astype(BF16)
    limit = dot(cap, one.astype(BF16))[0:1]
    kept = jnp.where(rank < limit, 1.0, 0.0)
    spill = two * (1.0 - kept)
    spill_rank = jnp.sum(dot(spill.astype(BF16), earlier) * spill, axis=0, keepdims=True)
    mine = one * kept
    n_kept = jnp.sum(mine, axis=1, keepdims=True)
    final = mine + spill
    n_all = jnp.sum(final, axis=1, keepdims=True)
    e0, e1 = iota((count, count), 0), iota((count, count), 1)
    wide = jnp.broadcast_to(n_all, (count, count)).astype(BF16)
    start = dot(ones_where((e1 < e0) & (e1 // CHUNK == e0 // CHUNK)), wide)
    fullest = jnp.max(dot(ones_where(e1 // CHUNK == e0 // CHUNK), wide))
    over = jnp.where(fullest > BIN - 1, 1.0, 0.0)
    for c in range(chunks):
        here = e0 % held // CHUNK == c
        value = jnp.where(e1 == e0 % CHUNK, n_all, jnp.where(e1 == CHUNK, over, 0.0))
        meta_ref[c] = jnp.where(here, value, 0.0).astype(BF16)
    place = jnp.sum(final * start[:, 0:1] + spill * n_kept, axis=0, keepdims=True)
    place = place + jnp.where(kept > 0.5, rank, spill_rank)
    chosen = jnp.where(kept > 0.5, first, backup)
    bins = chosen % held // CHUNK * (count // held) + chosen // held
    row = jnp.where(place < BIN - 1, bins.astype(F32) * BIN + place, -1.0)
    first_line = iota((8, toks), 0) == 0
    row_ref[...] = jnp.where(first_line, jnp.broadcast_to(row, (8, toks)), jnp.broadcast_to(gate_ref[...], (8, toks)))


def route(first, backup, capacity, gate, held):
    toks, count = first.shape[1], capacity.shape[1]
    return pl.pallas_call(
        functools.partial(route_kernel, held),
        out_shape=(
            jax.ShapeDtypeStruct((8, toks), F32),
            jax.ShapeDtypeStruct((held // CHUNK, count, count), BF16),
        ),
        compiler_params=params(),
        cost_estimate=cost(4 * toks * toks * count, toks * 512),
        name="route",
    )(first, backup, capacity, gate)


def dispatch_kernel(chunk, held, row_ref, tok_ref, meta_ref, out_ref):
    rows, toks = out_ref.shape[0], tok_ref.shape[0]
    count = meta_ref.shape[1]
    begin = pl.program_id(0) * rows
    at = iota((rows, toks), 0) + (begin + chunk * (count // held) * BIN)
    value = dot(ones_where(at == row_ref[0:1, :].astype(jnp.int32)), tok_ref[...])
    out_ref[...] = value.astype(BF16)
    at = iota((rows, count), 0) + begin
    spare = ones_where((at % BIN == BIN - 1) & (at // BIN == iota((rows, count), 1) // held))
    out_ref[:, 0:count] = (value[:, 0:count] + dot(spare, meta_ref[0])).astype(BF16)


def dispatch(row, tokens, meta, chunk, held):
    toks, wide = tokens.shape
    count = meta.shape[1]
    total = count // held * BIN
    block = total // 2
    return pl.pallas_call(
        functools.partial(dispatch_kernel, chunk, held),
        out_shape=jax.ShapeDtypeStruct((total, wide), BF16),
        grid=(total // block,),
        in_specs=[
            pl.BlockSpec((8, toks), lambda i: (0, 0)),
            pl.BlockSpec((toks, wide), lambda i: (0, 0)),
            pl.BlockSpec((1, count, count), lambda i: (chunk, 0, 0)),
        ],
        out_specs=pl.BlockSpec((block, wide), lambda i: (i, 0)),
        compiler_params=params(),
        cost_estimate=cost(2 * total * toks * wide, 2 * (total + toks) * wide),
        name="dispatch",
    )(row, tokens, meta)


def places_kernel(arrived_ref, row_ref, over_ref, top_ref):
    total = arrived_ref.shape[0]
    sources = total // BIN
    spare = ones_where(iota((sources, total), 1) == iota((sources, total), 0) * BIN + (BIN - 1))
    meta = dot(spare, arrived_ref[...]).astype(BF16)
    lane = ones_where(iota((8, 128), 0) == iota((8, 128), 1))
    told = dot_nt(lane, meta)
    n = jnp.where(iota((8, sources), 0) < CHUNK, told, 0.0)
    flagged = jnp.max(jnp.where(iota((8, sources), 0) == CHUNK, told, 0.0))
    each = jnp.sum(n, axis=1, keepdims=True)
    full = (jnp.max(each) > REACH - 1) | (jnp.sum(each) > LIST - 2)
    over = jnp.where((flagged > 0.5) | full, 1.0, 0.0)
    over_ref[...] = jnp.broadcast_to(over, (8, 128))
    top = jnp.broadcast_to(each[0:1] + 1.0, (8, 128))
    high = jnp.floor(top * (1.0 / 128.0))
    lane = iota((8, 128), 1)
    top_ref[...] = jnp.where(lane == 0, high, jnp.where(lane == 1, top - high * 128.0, 0.0))
    base = dot(n.astype(BF16), ones_where(iota((sources, sources), 0) < iota((sources, sources), 1)))
    begin = jnp.zeros((8, sources), F32)
    for j in range(CHUNK):
        ahead = iota((8, sources), 0) > j
        begin = begin + jnp.where(ahead, jnp.broadcast_to(n[j : j + 1], (8, sources)), 0.0)
    shift = base - begin + 128.0
    high = jnp.floor(shift * (1.0 / 128.0))
    low = shift - high * 128.0
    spread = ones_where(iota((sources, total), 1) // BIN == iota((sources, total), 0))
    place = dot(high.astype(BF16), spread) * 128.0 + dot(low.astype(BF16), spread) - 128.0
    begin = dot(begin.astype(BF16), spread)
    end = begin + dot(n.astype(BF16), spread)
    r = (iota((8, total), 1) % BIN).astype(F32)
    place = place + r
    inside = (r >= begin) & (r < end) & (place < REACH - 1) & (r < BIN - 1)
    place = jnp.where(iota((8, total), 0) == 0, place + 1.0, LIST - 2.0 - place)
    index = jnp.where(inside, place + 1.0, 0.0)
    index = jnp.sum(index, axis=0, keepdims=True) - 1.0
    row_ref[...] = jnp.broadcast_to(index, (8, total))


def places(arrived):
    total = arrived.shape[0]
    return pl.pallas_call(
        places_kernel,
        out_shape=(
            jax.ShapeDtypeStruct((8, total), F32),
            jax.ShapeDtypeStruct((8, 128), F32),
            jax.ShapeDtypeStruct((8, 128), F32),
        ),
        grid=(1,),
        in_specs=[pl.BlockSpec((total, 128), lambda i: (0, 0))],
        out_specs=(
            pl.BlockSpec((8, total), lambda i: (0, 0)),
            pl.BlockSpec((8, 128), lambda i: (0, 0)),
            pl.BlockSpec((8, 128), lambda i: (0, 0)),
        ),
        compiler_params=params(),
        cost_estimate=cost(1 << 25, 1 << 19),
        name="places",
    )(arrived)


def regroup_kernel(first, index_ref, rows_ref, top_ref, out_ref):
    count, many = out_ref.shape[0], rows_ref.shape[0]
    begin = first + pl.program_id(0) * count
    here = iota((count, many), 0) + begin
    value = dot(ones_where(here == index_ref[0:1, :].astype(jnp.int32)), rows_ref[...])
    out_ref[...] = value.astype(BF16)
    at = iota((count, 128), 0) + begin
    spare = jnp.where((at == 0) | (at == LIST - 1), top_ref[0:1, :], 0.0)
    out_ref[:, 0:128] = (value[:, 0:128] + spare).astype(BF16)


def regroup(index, rows, top, part):
    many, wide = rows.shape
    first, count = part
    block = min(count, 480)
    return pl.pallas_call(
        functools.partial(regroup_kernel, first),
        out_shape=jax.ShapeDtypeStruct((count, wide), BF16),
        grid=(count // block,),
        in_specs=[
            pl.BlockSpec((8, many), lambda i: (0, 0)),
            pl.BlockSpec((many, wide), lambda i: (0, 0)),
            pl.BlockSpec((8, 128), lambda i: (0, 0)),
        ],
        out_specs=pl.BlockSpec((block, wide), lambda i: (i, 0)),
        compiler_params=params(),
        cost_estimate=cost(2 * count * many * wide, 2 * (count + many) * wide),
        name="regroup",
    )(index, rows, top)


def weights_kernel(first, in_ref, out_ref, both_ref, held_ref, read_sems, write_sems):
    reads, writes = [], []
    for k, ref in enumerate((in_ref, out_ref)):
        for i in range(CHUNK):
            at = k * CHUNK + i
            reads.append(pltpu.make_async_copy(ref.at[first + i], held_ref.at[at], read_sems.at[at]))
            writes.append(pltpu.make_async_copy(held_ref.at[at], both_ref.at[at], write_sems.at[at]))
    for read in reads:
        read.start()
    for read, write in zip(reads, writes):
        read.wait()
        write.start()
    for write in writes:
        write.wait()


def weights(w_in, w_out, first):
    _, wide, hid = w_in.shape
    shape = (2 * CHUNK, wide, hid)
    return pl.pallas_call(
        functools.partial(weights_kernel, first),
        out_shape=jax.ShapeDtypeStruct(shape, w_in.dtype),
        in_specs=[pl.BlockSpec(memory_space=pl.ANY)] * 2,
        out_specs=pl.BlockSpec(memory_space=pl.ANY),
        scratch_shapes=[
            pltpu.VMEM(shape, w_in.dtype),
            pltpu.SemaphoreType.DMA((2 * CHUNK,)),
            pltpu.SemaphoreType.DMA((2 * CHUNK,)),
        ],
        compiler_params=params(),
        cost_estimate=cost(1, 8 * CHUNK * wide * hid),
        name="weights",
    )(w_in, w_out)


def expert_kernel(parts, *refs):
    n = len(parts)
    rows_refs, weight_refs = refs[:n], refs[n : n + 4]
    part_refs, total_refs = refs[-2 * n : -n], refs[-n:]
    step = pl.program_id(0)
    at = 0 if parts[0][0] == 0 else parts[0][1] - 16
    lane, line = iota((16, 128), 1), iota((16, 128), 0)
    scale = jnp.where(lane == 0, 128.0, jnp.where(lane == 1, 1.0, 0.0))
    scale = jnp.where(line == (0 if at == 0 else 15), scale, 0.0)
    top = jnp.sum(rows_refs[0][at : at + 16, 0:128].astype(F32) * scale).astype(jnp.int32)

    def add(upper, begins):
        in0_ref, out0_ref, in1_ref, out1_ref = weight_refs
        reach = (0, REACH) if upper else (LIST - REACH, LIST)
        for (first, count), rows_ref, total_ref in zip(parts, rows_refs, total_refs):
            low, high = max(reach[0] - first, 0), min(reach[1] - first, count)
            if begins and low > 0:
                total_ref[0:low, :] = jnp.zeros((low, total_ref.shape[1]), F32)
            if begins and high < count:
                total_ref[high:count, :] = jnp.zeros((count - high, total_ref.shape[1]), F32)
            place = iota((high - low, 1), 0) + (first + low)
            mine = place < top if upper else place >= top
            rows = jnp.where(mine, rows_ref[low:high, :], jnp.zeros((), BF16))
            term = None
            for in_ref, out_ref in ((in0_ref, out0_ref), (in1_ref, out1_ref)):
                hidden = jnp.maximum(dot(rows, in_ref[0]), 0.0).astype(BF16)
                part = dot(hidden, out_ref[0])
                term = part if term is None else term + part
            total_ref[low:high, :] = term if begins else total_ref[low:high, :] + term

    for k in range(CHUNK):

        @pl.when(step == k)
        def _(k=k):
            add(k == 0, k == 0)
            if k == CHUNK - 1:
                for part_ref, total_ref in zip(part_refs, total_refs):
                    part_ref[...] = total_ref[...].astype(part_ref.dtype)


def expert(rows, parts, w_in, w_out, first, other, dtype, later_than=()):
    wide, hid = w_in.shape[1], w_in.shape[2]
    total = sum(count for _, count in parts)
    wholes = [pl.BlockSpec((count, wide), lambda i: (0, 0)) for _, count in parts]
    made = pl.pallas_call(
        functools.partial(expert_kernel, parts),
        out_shape=[jax.ShapeDtypeStruct((count, wide), dtype) for _, count in parts],
        grid=(CHUNK,),
        in_specs=wholes
        + [
            pl.BlockSpec((1, wide, hid), lambda i: (first + i, 0, 0)),
            pl.BlockSpec((1, hid, wide), lambda i: (first + i, 0, 0)),
            pl.BlockSpec((1, wide, hid), lambda i: (i, 0, 0)),
            pl.BlockSpec((1, hid, wide), lambda i: (CHUNK + i, 0, 0)),
        ]
        + [pl.BlockSpec(memory_space=pl.ANY)] * len(later_than),
        out_specs=wholes,
        scratch_shapes=[pltpu.VMEM((count, wide), F32) for _, count in parts],
        compiler_params=pltpu.CompilerParams(vmem_limit_bytes=32 * 1024 * 1024),
        cost_estimate=cost(8 * total * wide * hid, 8 * CHUNK * wide * hid + 6 * total * wide),
        name="expert",
    )(*rows, w_in, w_out, other, other, *later_than)
    return list(made)


def back_kernel(parts, index_ref, over_ref, *refs):
    n, out_ref = len(parts), refs[-1]
    rows = out_ref.shape[0]
    col = turned(index_ref[...])[:, 0:1].astype(jnp.int32)
    result = None
    for i, (first, count) in enumerate(parts):
        value = (refs[i][...] + refs[n + i][...].astype(F32)).astype(BF16)
        part = dot(ones_where(col - first == iota((rows, count), 1)), value)
        result = part if result is None else result + part
    out_ref[...] = result.astype(BF16)
    at = iota((rows, 128), 0) + pl.program_id(0) * rows
    flag = jnp.where(at % BIN == BIN - 1, over_ref[0:1, :], 0.0)
    out_ref[:, 0:128] = (result[:, 0:128] + flag).astype(BF16)


def back(index, own, sent, over, parts):
    total, wide = index.shape[1], own[0].shape[1]
    block = total // 2
    wholes = [pl.BlockSpec((count, wide), lambda i: (0, 0)) for _, count in parts]
    return pl.pallas_call(
        functools.partial(back_kernel, parts),
        out_shape=jax.ShapeDtypeStruct((total, wide), BF16),
        grid=(total // block,),
        in_specs=[
            pl.BlockSpec((8, block), lambda i: (0, i)),
            pl.BlockSpec((8, 128), lambda i: (0, 0)),
        ]
        + wholes * 2,
        out_specs=pl.BlockSpec((block, wide), lambda i: (i, 0)),
        compiler_params=params(),
        cost_estimate=cost(2 * total * LIST * wide, 2 * total * wide + 6 * LIST * wide),
        name="back",
    )(index, over, *own, *sent)


def combine_kernel(chunk, last, row_ref, returned_ref, *refs):
    out_ref = refs[-1] if last else refs[-2]
    rows, many = out_ref.shape[0], returned_ref.shape[0]
    cols = turned(row_ref[...])
    col = cols[:, 0:1].astype(jnp.int32) - chunk * many
    total = dot(ones_where(col == iota((rows, many), 1)), returned_ref[...])
    if chunk > 0:
        total = total + refs[0][...].astype(F32)
    if last:
        out_ref[...] = (total * cols[:, 1:2]).astype(BF16)
        return
    out_ref[...] = total.astype(BF16)
    spare = iota((many, 128), 0) % BIN == BIN - 1
    over = jnp.max(jnp.where(spare, returned_ref[:, 0:128].astype(F32), 0.0))
    refs[-1][...] = jnp.broadcast_to(over, (8, 128))


def combine(row, returned, chunk, last, so_far):
    toks, (many, wide) = row.shape[1], returned.shape
    block = toks // 2
    extra = [] if so_far is None else [so_far]
    tokens_out = (jax.ShapeDtypeStruct((toks, wide), BF16), pl.BlockSpec((block, wide), lambda i: (i, 0)))
    flag_out = (jax.ShapeDtypeStruct((8, 128), F32), pl.BlockSpec((8, 128), lambda i: (0, 0)))
    shapes, specs = zip(*([tokens_out] if last else [tokens_out, flag_out]))
    return pl.pallas_call(
        functools.partial(combine_kernel, chunk, last),
        out_shape=shapes,
        grid=(toks // block,),
        in_specs=[
            pl.BlockSpec((8, block), lambda i: (0, i)),
            pl.BlockSpec((many, wide), lambda i: (0, 0)),
        ]
        + [pl.BlockSpec((block, wide), lambda i: (i, 0))] * len(extra),
        out_specs=specs,
        compiler_params=params(),
        cost_estimate=cost(2 * toks * many * wide, 2 * (many + 2 * toks) * wide),
        name="combine",
    )(row, returned, *extra)


def assign(first, backup, capacity, count, slot):
    columns = jnp.arange(count, dtype=jnp.int32)
    where = jnp.arange(first.shape[0], dtype=jnp.int32)
    earlier = ones_where(where[None, :] < where[:, None])
    onehot = (first[:, None] == columns[None, :]).astype(F32)
    rank = jnp.sum(dot(earlier, onehot.astype(BF16)) * onehot, axis=1)
    limit = jnp.sum(onehot * capacity[None, :].astype(F32), axis=1)
    kept = rank < limit
    spill = jnp.where((backup[:, None] == columns[None, :]) & ~kept[:, None], 1.0, 0.0)
    spill_rank = jnp.sum(dot(earlier, spill.astype(BF16)) * spill, axis=1)
    final = jnp.where(kept, first, backup)
    slots = jnp.where(kept, rank, slot + spill_rank).astype(jnp.int32)
    return slots, final


def general(tokens, gate, first, backup, capacity, w_in, w_out):
    held = w_in.shape[0]
    owners = lax.axis_size(EXPERT)
    helpers = lax.axis_size("helper")
    experts = held * owners
    slot = max(6, 3 * tokens.shape[0] // (2 * experts))
    slots, final = assign(first, backup, capacity, experts, slot)
    wide = tokens.shape[1]
    buffer = jnp.zeros((experts, 2 * slot, wide), BF16).at[final, slots].set(tokens)
    buffer = buffer.reshape(owners, held * 2 * slot, wide)
    arrived = lax.all_to_all(buffer, EXPERT, 0, 0, tiled=True)
    arrived = arrived.reshape(owners, held, 2 * slot, wide)
    rows = [arrived[:, e].reshape(owners * 2 * slot, wide) for e in range(held)]
    totals = [jnp.zeros(r.shape, F32) for r in rows]
    for k in range(helpers):
        turn = [(i, (i + k) % helpers) for i in range(helpers)]
        some_in = lax.ppermute(w_in, "helper", turn) if k else w_in
        some_out = lax.ppermute(w_out, "helper", turn) if k else w_out
        for e in range(held):
            hidden = jnp.maximum(dot(rows[e], some_in[e]), 0.0).astype(BF16)
            totals[e] = totals[e] + dot(hidden, some_out[e]).astype(BF16).astype(F32)
    outputs = [t.astype(BF16).reshape(owners, 2 * slot, wide) for t in totals]
    result = jnp.stack(outputs, axis=1).reshape(owners, held * 2 * slot, wide)
    returned = lax.all_to_all(result, EXPERT, 0, 0, tiled=True)
    picked = returned.reshape(experts, 2 * slot, wide)[final, slots]
    return (gate[:, None] * picked.astype(F32)).astype(BF16)


def after(*values):
    return lax.optimization_barrier(values)


def on_device(tokens, gate, expert_ids, backup_ids, capacity, w_in, w_out):
    held = w_in.shape[0]
    owners = lax.axis_size(EXPERT)
    helpers = lax.axis_size("helper")
    toks, wide = tokens.shape
    chunks = range(held // CHUNK)
    w_parts = [weights(w_in, w_out, c * CHUNK) for c in chunks]
    others = [lax.ppermute(w, CORE_X, NEAR) for w in w_parts]
    row, meta = route(
        expert_ids.reshape(1, toks),
        backup_ids.reshape(1, toks),
        capacity.reshape(1, -1),
        gate.reshape(1, toks),
        held,
    )

    def exchange(rows):
        rows = lax.all_to_all(rows.reshape(owners, BIN, wide), EXPERT, 0, 0, tiled=True)
        return rows.reshape(owners * BIN, wide)

    arrived = [exchange(dispatch(row, tokens, meta, c, held)) for c in chunks]
    at_row, overs, tops = zip(*[places(a) for a in arrived])
    rows = [[regroup(at_row[c], arrived[c], tops[c], p) for p in PARTS[c]] for c in chunks]
    theirs = [[lax.ppermute(r, CORE_X, FAR) for r in rows[c]] for c in chunks]
    over = functools.reduce(jnp.maximum, overs)
    own, sent = [], []
    for c in chunks:
        k = c * CHUNK
        args = (w_in, w_out, k, others[c])
        made = [expert([t], [p], *args, BF16)[0] for t, p in zip(theirs[c], PARTS[c])]
        sent.append([lax.ppermute(m, CORE_X, FAR) for m in made])
        ahead = rows[c + 1] if c < chunks[-1] else []
        own.append(expert(rows[c], PARTS[c], *args, F32, ahead))
    mixed, flags = None, []
    for c in chunks:
        returned = exchange(back(at_row[c], own[c], sent[c], over, PARTS[c]))
        mixed, *flag = combine(row, returned, c, c == chunks[-1], mixed)
        flags += flag
    around = [[(i, (i + k) % helpers) for i in range(helpers)] for k in range(1, helpers)]
    over = functools.reduce(jnp.maximum, [flags[0]] + [lax.ppermute(flags[0], "helper", a) for a in around])
    again = (tokens, gate, expert_ids[:, 0], backup_ids[:, 0], capacity, w_in, w_out)
    _, mixed = lax.while_loop(
        lambda state: state[0] > 0.5,
        lambda state: (jnp.zeros_like(state[0]), general(*again)),
        (over[0, 0], mixed),
    )
    return mixed


def solution(mesh):
    torus = Mesh(
        mesh.devices.reshape(4, 4, 2, mesh.shape["helper"]),
        ("expert_0", "expert_1", "expert_2", "helper"),
    )
    in_specs = (
        P(EXPERT_HELPER, None),
        P(EXPERT_HELPER),
        P(EXPERT_HELPER, None),
        P(EXPERT_HELPER, None),
        P(),
        P(EXPERT, None, "helper"),
        P(EXPERT, "helper", None),
    )
    out_specs = P(EXPERT_HELPER, None)
    return jax.shard_map(
        on_device, mesh=torus, in_specs=in_specs, out_specs=out_specs, check_vma=False
    )
```

```python
import functools

import jax
import jax.numpy as jnp
from jax import lax
from jax.experimental import pallas as pl
from jax.experimental.pallas import tpu as pltpu
from jax.sharding import Mesh
from jax.sharding import PartitionSpec as P

EXPERT = ("expert_0", "expert_1", "expert_2")
EXPERT_HELPER = ("expert_0", "expert_1", "expert_2", "helper")
CHUNK = 2
BIN = 40
LIST = 960
REACH = 576
PARTS = (((0, 960),), ((0, 480), (480, 480)))
CORE_X = ("expert_2", "helper")
NEAR = [(0, 1), (1, 0), (2, 3), (3, 2), (5, 6), (6, 5), (7, 4), (4, 7)]
FAR = [(1, 2), (2, 1), (3, 0), (0, 3), (4, 5), (5, 4), (6, 7), (7, 6)]
F32 = jnp.float32
BF16 = jnp.bfloat16
VMEM_LIMIT = 24 * 1024 * 1024


def dot(a, b):
    return jnp.dot(a, b, preferred_element_type=F32)


def dot_nt(a, b):
    return lax.dot_general(a, b, (((1,), (1,)), ((), ())), preferred_element_type=F32)


def turned(rows):
    return jnp.concatenate([rows, jnp.zeros((120, rows.shape[1]), F32)], axis=0).T


def iota(shape, dim):
    return lax.broadcasted_iota(jnp.int32, shape, dim)


def ones_where(cond):
    return jnp.where(cond, 1.0, 0.0).astype(BF16)


def params():
    return pltpu.CompilerParams(vmem_limit_bytes=VMEM_LIMIT)


def cost(flops, read):
    return pl.CostEstimate(flops=flops, bytes_accessed=read, transcendentals=0)


def route_kernel(held, first_ref, backup_ref, cap_ref, gate_ref, row_ref, meta_ref):
    count = cap_ref.shape[1]
    toks = first_ref.shape[1]
    chunks = held // CHUNK
    ids = iota((count, toks), 0)
    first = first_ref[...]
    backup = backup_ref[...]
    one = jnp.where(ids == first, 1.0, 0.0)
    two = jnp.where(ids == backup, 1.0, 0.0)
    earlier = ones_where(iota((toks, toks), 0) < iota((toks, toks), 1))
    rank = jnp.sum(dot(one.astype(BF16), earlier) * one, axis=0, keepdims=True)
    cap = jnp.broadcast_to(cap_ref[...].astype(F32), (8, count)).astype(BF16)
    limit = dot(cap, one.astype(BF16))[0:1]
    kept = jnp.where(rank < limit, 1.0, 0.0)
    spill = two * (1.0 - kept)
    spill_rank = jnp.sum(dot(spill.astype(BF16), earlier) * spill, axis=0, keepdims=True)
    mine = one * kept
    n_kept = jnp.sum(mine, axis=1, keepdims=True)
    final = mine + spill
    n_all = jnp.sum(final, axis=1, keepdims=True)
    e0, e1 = iota((count, count), 0), iota((count, count), 1)
    wide = jnp.broadcast_to(n_all, (count, count)).astype(BF16)
    start = dot(ones_where((e1 < e0) & (e1 // CHUNK == e0 // CHUNK)), wide)
    fullest = jnp.max(dot(ones_where(e1 // CHUNK == e0 // CHUNK), wide))
    over = jnp.where(fullest > BIN - 1, 1.0, 0.0)
    for c in range(chunks):
        here = e0 % held // CHUNK == c
        value = jnp.where(e1 == e0 % CHUNK, n_all, jnp.where(e1 == CHUNK, over, 0.0))
        meta_ref[c] = jnp.where(here, value, 0.0).astype(BF16)
    place = jnp.sum(final * start[:, 0:1] + spill * n_kept, axis=0, keepdims=True)
    place = place + jnp.where(kept > 0.5, rank, spill_rank)
    chosen = jnp.where(kept > 0.5, first, backup)
    bins = chosen % held // CHUNK * (count // held) + chosen // held
    row = jnp.where(place < BIN - 1, bins.astype(F32) * BIN + place, -1.0)
    first_line = iota((8, toks), 0) == 0
    row_ref[...] = jnp.where(first_line, jnp.broadcast_to(row, (8, toks)), jnp.broadcast_to(gate_ref[...], (8, toks)))


def route(first, backup, capacity, gate, held):
    toks, count = first.shape[1], capacity.shape[1]
    return pl.pallas_call(
        functools.partial(route_kernel, held),
        out_shape=(
            jax.ShapeDtypeStruct((8, toks), F32),
            jax.ShapeDtypeStruct((held // CHUNK, count, count), BF16),
        ),
        compiler_params=params(),
        cost_estimate=cost(4 * toks * toks * count, toks * 512),
        name="route",
    )(first, backup, capacity, gate)


def dispatch_kernel(chunk, held, row_ref, tok_ref, meta_ref, out_ref):
    rows, toks = out_ref.shape[0], tok_ref.shape[0]
    count = meta_ref.shape[1]
    begin = pl.program_id(0) * rows
    at = iota((rows, toks), 0) + (begin + chunk * (count // held) * BIN)
    value = dot(ones_where(at == row_ref[0:1, :].astype(jnp.int32)), tok_ref[...])
    out_ref[...] = value.astype(BF16)
    at = iota((rows, count), 0) + begin
    spare = ones_where((at % BIN == BIN - 1) & (at // BIN == iota((rows, count), 1) // held))
    out_ref[:, 0:count] = (value[:, 0:count] + dot(spare, meta_ref[0])).astype(BF16)


def dispatch(row, tokens, meta, chunk, held):
    toks, wide = tokens.shape
    count = meta.shape[1]
    total = count // held * BIN
    block = total // 2
    return pl.pallas_call(
        functools.partial(dispatch_kernel, chunk, held),
        out_shape=jax.ShapeDtypeStruct((total, wide), BF16),
        grid=(total // block,),
        in_specs=[
            pl.BlockSpec((8, toks), lambda i: (0, 0)),
            pl.BlockSpec((toks, wide), lambda i: (0, 0)),
            pl.BlockSpec((1, count, count), lambda i: (chunk, 0, 0)),
        ],
        out_specs=pl.BlockSpec((block, wide), lambda i: (i, 0)),
        compiler_params=params(),
        cost_estimate=cost(2 * total * toks * wide, 2 * (total + toks) * wide),
        name="dispatch",
    )(row, tokens, meta)


def places_kernel(arrived_ref, row_ref, over_ref, top_ref):
    total = arrived_ref.shape[0]
    sources = total // BIN
    spare = ones_where(iota((sources, total), 1) == iota((sources, total), 0) * BIN + (BIN - 1))
    meta = dot(spare, arrived_ref[...]).astype(BF16)
    lane = ones_where(iota((8, 128), 0) == iota((8, 128), 1))
    told = dot_nt(lane, meta)
    n = jnp.where(iota((8, sources), 0) < CHUNK, told, 0.0)
    flagged = jnp.max(jnp.where(iota((8, sources), 0) == CHUNK, told, 0.0))
    each = jnp.sum(n, axis=1, keepdims=True)
    full = (jnp.max(each) > REACH - 1) | (jnp.sum(each) > LIST - 2)
    over = jnp.where((flagged > 0.5) | full, 1.0, 0.0)
    over_ref[...] = jnp.broadcast_to(over, (8, 128))
    top = jnp.broadcast_to(each[0:1] + 1.0, (8, 128))
    high = jnp.floor(top * (1.0 / 128.0))
    lane = iota((8, 128), 1)
    top_ref[...] = jnp.where(lane == 0, high, jnp.where(lane == 1, top - high * 128.0, 0.0))
    base = dot(n.astype(BF16), ones_where(iota((sources, sources), 0) < iota((sources, sources), 1)))
    begin = jnp.zeros((8, sources), F32)
    for j in range(CHUNK):
        ahead = iota((8, sources), 0) > j
        begin = begin + jnp.where(ahead, jnp.broadcast_to(n[j : j + 1], (8, sources)), 0.0)
    shift = base - begin + 128.0
    high = jnp.floor(shift * (1.0 / 128.0))
    low = shift - high * 128.0
    spread = ones_where(iota((sources, total), 1) // BIN == iota((sources, total), 0))
    place = dot(high.astype(BF16), spread) * 128.0 + dot(low.astype(BF16), spread) - 128.0
    begin = dot(begin.astype(BF16), spread)
    end = begin + dot(n.astype(BF16), spread)
    r = (iota((8, total), 1) % BIN).astype(F32)
    place = place + r
    inside = (r >= begin) & (r < end) & (place < REACH - 1) & (r < BIN - 1)
    place = jnp.where(iota((8, total), 0) == 0, place + 1.0, LIST - 2.0 - place)
    index = jnp.where(inside, place + 1.0, 0.0)
    index = jnp.sum(index, axis=0, keepdims=True) - 1.0
    row_ref[...] = jnp.broadcast_to(index, (8, total))


def places(arrived):
    total = arrived.shape[0]
    return pl.pallas_call(
        places_kernel,
        out_shape=(
            jax.ShapeDtypeStruct((8, total), F32),
            jax.ShapeDtypeStruct((8, 128), F32),
            jax.ShapeDtypeStruct((8, 128), F32),
        ),
        grid=(1,),
        in_specs=[pl.BlockSpec((total, 128), lambda i: (0, 0))],
        out_specs=(
            pl.BlockSpec((8, total), lambda i: (0, 0)),
            pl.BlockSpec((8, 128), lambda i: (0, 0)),
            pl.BlockSpec((8, 128), lambda i: (0, 0)),
        ),
        compiler_params=params(),
        cost_estimate=cost(1 << 25, 1 << 19),
        name="places",
    )(arrived)


def regroup_kernel(first, index_ref, rows_ref, top_ref, out_ref):
    count, many = out_ref.shape[0], rows_ref.shape[0]
    begin = first + pl.program_id(0) * count
    here = iota((count, many), 0) + begin
    value = dot(ones_where(here == index_ref[0:1, :].astype(jnp.int32)), rows_ref[...])
    out_ref[...] = value.astype(BF16)
    at = iota((count, 128), 0) + begin
    spare = jnp.where((at == 0) | (at == LIST - 1), top_ref[0:1, :], 0.0)
    out_ref[:, 0:128] = (value[:, 0:128] + spare).astype(BF16)


def regroup(index, rows, top, part):
    many, wide = rows.shape
    first, count = part
    block = min(count, 480)
    return pl.pallas_call(
        functools.partial(regroup_kernel, first),
        out_shape=jax.ShapeDtypeStruct((count, wide), BF16),
        grid=(count // block,),
        in_specs=[
            pl.BlockSpec((8, many), lambda i: (0, 0)),
            pl.BlockSpec((many, wide), lambda i: (0, 0)),
            pl.BlockSpec((8, 128), lambda i: (0, 0)),
        ],
        out_specs=pl.BlockSpec((block, wide), lambda i: (i, 0)),
        compiler_params=params(),
        cost_estimate=cost(2 * count * many * wide, 2 * (count + many) * wide),
        name="regroup",
    )(index, rows, top)


def weights_kernel(first, in_ref, out_ref, both_ref, held_ref, read_sems, write_sems):
    reads, writes = [], []
    for k, ref in enumerate((in_ref, out_ref)):
        for i in range(CHUNK):
            at = k * CHUNK + i
            reads.append(pltpu.make_async_copy(ref.at[first + i], held_ref.at[at], read_sems.at[at]))
            writes.append(pltpu.make_async_copy(held_ref.at[at], both_ref.at[at], write_sems.at[at]))
    for read in reads:
        read.start()
    for read, write in zip(reads, writes):
        read.wait()
        write.start()
    for write in writes:
        write.wait()


def weights(w_in, w_out, first):
    _, wide, hid = w_in.shape
    shape = (2 * CHUNK, wide, hid)
    return pl.pallas_call(
        functools.partial(weights_kernel, first),
        out_shape=jax.ShapeDtypeStruct(shape, w_in.dtype),
        in_specs=[pl.BlockSpec(memory_space=pl.ANY)] * 2,
        out_specs=pl.BlockSpec(memory_space=pl.ANY),
        scratch_shapes=[
            pltpu.VMEM(shape, w_in.dtype),
            pltpu.SemaphoreType.DMA((2 * CHUNK,)),
            pltpu.SemaphoreType.DMA((2 * CHUNK,)),
        ],
        compiler_params=params(),
        cost_estimate=cost(1, 8 * CHUNK * wide * hid),
        name="weights",
    )(w_in, w_out)


def expert_kernel(parts, *refs):
    n = len(parts)
    rows_refs, weight_refs = refs[:n], refs[n : n + 4]
    part_refs, total_refs = refs[-2 * n : -n], refs[-n:]
    step = pl.program_id(0)
    at = 0 if parts[0][0] == 0 else parts[0][1] - 16
    lane, line = iota((16, 128), 1), iota((16, 128), 0)
    scale = jnp.where(lane == 0, 128.0, jnp.where(lane == 1, 1.0, 0.0))
    scale = jnp.where(line == (0 if at == 0 else 15), scale, 0.0)
    top = jnp.sum(rows_refs[0][at : at + 16, 0:128].astype(F32) * scale).astype(jnp.int32)

    def add(upper, begins):
        in0_ref, out0_ref, in1_ref, out1_ref = weight_refs
        reach = (0, REACH) if upper else (LIST - REACH, LIST)
        for (first, count), rows_ref, total_ref in zip(parts, rows_refs, total_refs):
            low, high = max(reach[0] - first, 0), min(reach[1] - first, count)
            if begins and low > 0:
                total_ref[0:low, :] = jnp.zeros((low, total_ref.shape[1]), F32)
            if begins and high < count:
                total_ref[high:count, :] = jnp.zeros((count - high, total_ref.shape[1]), F32)
            place = iota((high - low, 1), 0) + (first + low)
            mine = place < top if upper else place >= top
            rows = jnp.where(mine, rows_ref[low:high, :], jnp.zeros((), BF16))
            term = None
            for in_ref, out_ref in ((in0_ref, out0_ref), (in1_ref, out1_ref)):
                hidden = jnp.maximum(dot(rows, in_ref[0]), 0.0).astype(BF16)
                part = dot(hidden, out_ref[0])
                term = part if term is None else term + part
            total_ref[low:high, :] = term if begins else total_ref[low:high, :] + term

    for k in range(CHUNK):

        @pl.when(step == k)
        def _(k=k):
            add(k == 0, k == 0)
            if k == CHUNK - 1:
                for part_ref, total_ref in zip(part_refs, total_refs):
                    part_ref[...] = total_ref[...].astype(part_ref.dtype)


def expert(rows, parts, w_in, w_out, first, other, dtype, later_than=()):
    wide, hid = w_in.shape[1], w_in.shape[2]
    total = sum(count for _, count in parts)
    wholes = [pl.BlockSpec((count, wide), lambda i: (0, 0)) for _, count in parts]
    made = pl.pallas_call(
        functools.partial(expert_kernel, parts),
        out_shape=[jax.ShapeDtypeStruct((count, wide), dtype) for _, count in parts],
        grid=(CHUNK,),
        in_specs=wholes
        + [
            pl.BlockSpec((1, wide, hid), lambda i: (first + i, 0, 0)),
            pl.BlockSpec((1, hid, wide), lambda i: (first + i, 0, 0)),
            pl.BlockSpec((1, wide, hid), lambda i: (i, 0, 0)),
            pl.BlockSpec((1, hid, wide), lambda i: (CHUNK + i, 0, 0)),
        ]
        + [pl.BlockSpec(memory_space=pl.ANY)] * len(later_than),
        out_specs=wholes,
        scratch_shapes=[pltpu.VMEM((count, wide), F32) for _, count in parts],
        compiler_params=pltpu.CompilerParams(vmem_limit_bytes=32 * 1024 * 1024),
        cost_estimate=cost(8 * total * wide * hid, 8 * CHUNK * wide * hid + 6 * total * wide),
        name="expert",
    )(*rows, w_in, w_out, other, other, *later_than)
    return list(made)


def back_kernel(parts, index_ref, over_ref, *refs):
    n, out_ref = len(parts), refs[-1]
    rows = out_ref.shape[0]
    col = turned(index_ref[...])[:, 0:1].astype(jnp.int32)
    result = None
    for i, (first, count) in enumerate(parts):
        value = (refs[i][...] + refs[n + i][...].astype(F32)).astype(BF16)
        part = dot(ones_where(col - first == iota((rows, count), 1)), value)
        result = part if result is None else result + part
    out_ref[...] = result.astype(BF16)
    at = iota((rows, 128), 0) + pl.program_id(0) * rows
    flag = jnp.where(at % BIN == BIN - 1, over_ref[0:1, :], 0.0)
    out_ref[:, 0:128] = (result[:, 0:128] + flag).astype(BF16)


def back(index, own, sent, over, parts):
    total, wide = index.shape[1], own[0].shape[1]
    block = total // 2
    wholes = [pl.BlockSpec((count, wide), lambda i: (0, 0)) for _, count in parts]
    return pl.pallas_call(
        functools.partial(back_kernel, parts),
        out_shape=jax.ShapeDtypeStruct((total, wide), BF16),
        grid=(total // block,),
        in_specs=[
            pl.BlockSpec((8, block), lambda i: (0, i)),
            pl.BlockSpec((8, 128), lambda i: (0, 0)),
        ]
        + wholes * 2,
        out_specs=pl.BlockSpec((block, wide), lambda i: (i, 0)),
        compiler_params=params(),
        cost_estimate=cost(2 * total * LIST * wide, 2 * total * wide + 6 * LIST * wide),
        name="back",
    )(index, over, *own, *sent)


def combine_kernel(chunk, last, row_ref, returned_ref, *refs):
    out_ref = refs[-1] if last else refs[-2]
    rows, many = out_ref.shape[0], returned_ref.shape[0]
    cols = turned(row_ref[...])
    col = cols[:, 0:1].astype(jnp.int32) - chunk * many
    total = dot(ones_where(col == iota((rows, many), 1)), returned_ref[...])
    if chunk > 0:
        total = total + refs[0][...].astype(F32)
    if last:
        out_ref[...] = (total * cols[:, 1:2]).astype(BF16)
        return
    out_ref[...] = total.astype(BF16)
    spare = iota((many, 128), 0) % BIN == BIN - 1
    over = jnp.max(jnp.where(spare, returned_ref[:, 0:128].astype(F32), 0.0))
    refs[-1][...] = jnp.broadcast_to(over, (8, 128))


def combine(row, returned, chunk, last, so_far):
    toks, (many, wide) = row.shape[1], returned.shape
    block = toks // 2
    extra = [] if so_far is None else [so_far]
    tokens_out = (jax.ShapeDtypeStruct((toks, wide), BF16), pl.BlockSpec((block, wide), lambda i: (i, 0)))
    flag_out = (jax.ShapeDtypeStruct((8, 128), F32), pl.BlockSpec((8, 128), lambda i: (0, 0)))
    shapes, specs = zip(*([tokens_out] if last else [tokens_out, flag_out]))
    return pl.pallas_call(
        functools.partial(combine_kernel, chunk, last),
        out_shape=shapes,
        grid=(toks // block,),
        in_specs=[
            pl.BlockSpec((8, block), lambda i: (0, i)),
            pl.BlockSpec((many, wide), lambda i: (0, 0)),
        ]
        + [pl.BlockSpec((block, wide), lambda i: (i, 0))] * len(extra),
        out_specs=specs,
        compiler_params=params(),
        cost_estimate=cost(2 * toks * many * wide, 2 * (many + 2 * toks) * wide),
        name="combine",
    )(row, returned, *extra)


def assign(first, backup, capacity, count, slot):
    columns = jnp.arange(count, dtype=jnp.int32)
    where = jnp.arange(first.shape[0], dtype=jnp.int32)
    earlier = ones_where(where[None, :] < where[:, None])
    onehot = (first[:, None] == columns[None, :]).astype(F32)
    rank = jnp.sum(dot(earlier, onehot.astype(BF16)) * onehot, axis=1)
    limit = jnp.sum(onehot * capacity[None, :].astype(F32), axis=1)
    kept = rank < limit
    spill = jnp.where((backup[:, None] == columns[None, :]) & ~kept[:, None], 1.0, 0.0)
    spill_rank = jnp.sum(dot(earlier, spill.astype(BF16)) * spill, axis=1)
    final = jnp.where(kept, first, backup)
    slots = jnp.where(kept, rank, slot + spill_rank).astype(jnp.int32)
    return slots, final


def general(tokens, gate, first, backup, capacity, w_in, w_out):
    held = w_in.shape[0]
    owners = lax.axis_size(EXPERT)
    helpers = lax.axis_size("helper")
    experts = held * owners
    slot = max(6, 3 * tokens.shape[0] // (2 * experts))
    slots, final = assign(first, backup, capacity, experts, slot)
    wide = tokens.shape[1]
    buffer = jnp.zeros((experts, 2 * slot, wide), BF16).at[final, slots].set(tokens)
    buffer = buffer.reshape(owners, held * 2 * slot, wide)
    arrived = lax.all_to_all(buffer, EXPERT, 0, 0, tiled=True)
    arrived = arrived.reshape(owners, held, 2 * slot, wide)
    rows = [arrived[:, e].reshape(owners * 2 * slot, wide) for e in range(held)]
    totals = [jnp.zeros(r.shape, F32) for r in rows]
    for k in range(helpers):
        turn = [(i, (i + k) % helpers) for i in range(helpers)]
        some_in = lax.ppermute(w_in, "helper", turn) if k else w_in
        some_out = lax.ppermute(w_out, "helper", turn) if k else w_out
        for e in range(held):
            hidden = jnp.maximum(dot(rows[e], some_in[e]), 0.0).astype(BF16)
            totals[e] = totals[e] + dot(hidden, some_out[e]).astype(BF16).astype(F32)
    outputs = [t.astype(BF16).reshape(owners, 2 * slot, wide) for t in totals]
    result = jnp.stack(outputs, axis=1).reshape(owners, held * 2 * slot, wide)
    returned = lax.all_to_all(result, EXPERT, 0, 0, tiled=True)
    picked = returned.reshape(experts, 2 * slot, wide)[final, slots]
    return (gate[:, None] * picked.astype(F32)).astype(BF16)


def after(*values):
    return lax.optimization_barrier(values)


def on_device(tokens, gate, expert_ids, backup_ids, capacity, w_in, w_out):
    held = w_in.shape[0]
    owners = lax.axis_size(EXPERT)
    helpers = lax.axis_size("helper")
    toks, wide = tokens.shape
    chunks = range(held // CHUNK)
    w_parts = [weights(w_in, w_out, c * CHUNK) for c in chunks]
    others = [lax.ppermute(w, CORE_X, NEAR) for w in w_parts]
    row, meta = route(
        expert_ids.reshape(1, toks),
        backup_ids.reshape(1, toks),
        capacity.reshape(1, -1),
        gate.reshape(1, toks),
        held,
    )

    def exchange(rows):
        rows = lax.all_to_all(rows.reshape(owners, BIN, wide), EXPERT, 0, 0, tiled=True)
        return rows.reshape(owners * BIN, wide)

    arrived = [exchange(dispatch(row, tokens, meta, c, held)) for c in chunks]
    at_row, overs, tops = zip(*[places(a) for a in arrived])
    rows = [[regroup(at_row[c], arrived[c], tops[c], p) for p in PARTS[c]] for c in chunks]
    theirs = [[lax.ppermute(r, CORE_X, FAR) for r in rows[c]] for c in chunks]
    over = functools.reduce(jnp.maximum, overs)
    own, sent = [], []
    for c in chunks:
        k = c * CHUNK
        args = (w_in, w_out, k, others[c])
        made = [expert([t], [p], *args, BF16)[0] for t, p in zip(theirs[c], PARTS[c])]
        sent.append([lax.ppermute(m, CORE_X, FAR) for m in made])
        ahead = rows[c + 1] if c < chunks[-1] else []
        own.append(expert(rows[c], PARTS[c], *args, F32, ahead))
    mixed, flags = None, []
    for c in chunks:
        returned = exchange(back(at_row[c], own[c], sent[c], over, PARTS[c]))
        mixed, *flag = combine(row, returned, c, c == chunks[-1], mixed)
        flags += flag
    around = [[(i, (i + k) % helpers) for i in range(helpers)] for k in range(1, helpers)]
    over = functools.reduce(jnp.maximum, [flags[0]] + [lax.ppermute(flags[0], "helper", a) for a in around])
    return lax.cond(
        over[0, 0] > 0.5,
        lambda ops: general(*ops[1:]),
        lambda ops: ops[0],
        (mixed, tokens, gate, expert_ids[:, 0], backup_ids[:, 0], capacity, w_in, w_out),
    )


def solution(mesh):
    torus = Mesh(
        mesh.devices.reshape(4, 4, 2, mesh.shape["helper"]),
        ("expert_0", "expert_1", "expert_2", "helper"),
    )
    in_specs = (
        P(EXPERT_HELPER, None),
        P(EXPERT_HELPER),
        P(EXPERT_HELPER, None),
        P(EXPERT_HELPER, None),
        P(),
        P(EXPERT, None, "helper"),
        P(EXPERT, "helper", None),
    )
    out_specs = P(EXPERT_HELPER, None)
    return jax.shard_map(
        on_device, mesh=torus, in_specs=in_specs, out_specs=out_specs, check_vma=False
    )
```

```python
import functools

import jax
import jax.numpy as jnp
from jax import lax
from jax.experimental import pallas as pl
from jax.experimental.pallas import tpu as pltpu
from jax.sharding import Mesh
from jax.sharding import PartitionSpec as P

EXPERT = ("expert_0", "expert_1", "expert_2")
EXPERT_HELPER = ("expert_0", "expert_1", "expert_2", "helper")
CHUNK = 2
BIN = 40
LIST = 960
REACH = 576
PARTS = (((0, 960),), ((0, 560), (560, 400)))
CORE_X = ("expert_2", "helper")
NEAR = [(0, 1), (1, 0), (2, 3), (3, 2), (5, 6), (6, 5), (7, 4), (4, 7)]
FAR = [(1, 2), (2, 1), (3, 0), (0, 3), (4, 5), (5, 4), (6, 7), (7, 6)]
F32 = jnp.float32
BF16 = jnp.bfloat16
VMEM_LIMIT = 24 * 1024 * 1024


def dot(a, b):
    return jnp.dot(a, b, preferred_element_type=F32)


def dot_nt(a, b):
    return lax.dot_general(a, b, (((1,), (1,)), ((), ())), preferred_element_type=F32)


def turned(rows):
    return jnp.concatenate([rows, jnp.zeros((120, rows.shape[1]), F32)], axis=0).T


def iota(shape, dim):
    return lax.broadcasted_iota(jnp.int32, shape, dim)


def ones_where(cond):
    return jnp.where(cond, 1.0, 0.0).astype(BF16)


def params():
    return pltpu.CompilerParams(vmem_limit_bytes=VMEM_LIMIT)


def cost(flops, read):
    return pl.CostEstimate(flops=flops, bytes_accessed=read, transcendentals=0)


def route_kernel(held, first_ref, backup_ref, cap_ref, gate_ref, row_ref, meta_ref):
    count = cap_ref.shape[1]
    toks = first_ref.shape[1]
    chunks = held // CHUNK
    ids = iota((count, toks), 0)
    first = first_ref[...]
    backup = backup_ref[...]
    one = jnp.where(ids == first, 1.0, 0.0)
    two = jnp.where(ids == backup, 1.0, 0.0)
    earlier = ones_where(iota((toks, toks), 0) < iota((toks, toks), 1))
    rank = jnp.sum(dot(one.astype(BF16), earlier) * one, axis=0, keepdims=True)
    cap = jnp.broadcast_to(cap_ref[...].astype(F32), (8, count)).astype(BF16)
    limit = dot(cap, one.astype(BF16))[0:1]
    kept = jnp.where(rank < limit, 1.0, 0.0)
    spill = two * (1.0 - kept)
    spill_rank = jnp.sum(dot(spill.astype(BF16), earlier) * spill, axis=0, keepdims=True)
    mine = one * kept
    n_kept = jnp.sum(mine, axis=1, keepdims=True)
    final = mine + spill
    n_all = jnp.sum(final, axis=1, keepdims=True)
    e0, e1 = iota((count, count), 0), iota((count, count), 1)
    wide = jnp.broadcast_to(n_all, (count, count)).astype(BF16)
    start = dot(ones_where((e1 < e0) & (e1 // CHUNK == e0 // CHUNK)), wide)
    fullest = jnp.max(dot(ones_where(e1 // CHUNK == e0 // CHUNK), wide))
    over = jnp.where(fullest > BIN - 1, 1.0, 0.0)
    for c in range(chunks):
        here = e0 % held // CHUNK == c
        value = jnp.where(e1 == e0 % CHUNK, n_all, jnp.where(e1 == CHUNK, over, 0.0))
        meta_ref[c] = jnp.where(here, value, 0.0).astype(BF16)
    place = jnp.sum(final * start[:, 0:1] + spill * n_kept, axis=0, keepdims=True)
    place = place + jnp.where(kept > 0.5, rank, spill_rank)
    chosen = jnp.where(kept > 0.5, first, backup)
    bins = chosen % held // CHUNK * (count // held) + chosen // held
    row = jnp.where(place < BIN - 1, bins.astype(F32) * BIN + place, -1.0)
    first_line = iota((8, toks), 0) == 0
    row_ref[...] = jnp.where(first_line, jnp.broadcast_to(row, (8, toks)), jnp.broadcast_to(gate_ref[...], (8, toks)))


def route(first, backup, capacity, gate, held):
    toks, count = first.shape[1], capacity.shape[1]
    return pl.pallas_call(
        functools.partial(route_kernel, held),
        out_shape=(
            jax.ShapeDtypeStruct((8, toks), F32),
            jax.ShapeDtypeStruct((held // CHUNK, count, count), BF16),
        ),
        compiler_params=params(),
        cost_estimate=cost(4 * toks * toks * count, toks * 512),
        name="route",
    )(first, backup, capacity, gate)


def dispatch_kernel(chunk, held, row_ref, tok_ref, meta_ref, out_ref):
    rows, toks = out_ref.shape[0], tok_ref.shape[0]
    count = meta_ref.shape[1]
    begin = pl.program_id(0) * rows
    at = iota((rows, toks), 0) + (begin + chunk * (count // held) * BIN)
    value = dot(ones_where(at == row_ref[0:1, :].astype(jnp.int32)), tok_ref[...])
    out_ref[...] = value.astype(BF16)
    at = iota((rows, count), 0) + begin
    spare = ones_where((at % BIN == BIN - 1) & (at // BIN == iota((rows, count), 1) // held))
    out_ref[:, 0:count] = (value[:, 0:count] + dot(spare, meta_ref[0])).astype(BF16)


def dispatch(row, tokens, meta, chunk, held):
    toks, wide = tokens.shape
    count = meta.shape[1]
    total = count // held * BIN
    block = total // 2
    return pl.pallas_call(
        functools.partial(dispatch_kernel, chunk, held),
        out_shape=jax.ShapeDtypeStruct((total, wide), BF16),
        grid=(total // block,),
        in_specs=[
            pl.BlockSpec((8, toks), lambda i: (0, 0)),
            pl.BlockSpec((toks, wide), lambda i: (0, 0)),
            pl.BlockSpec((1, count, count), lambda i: (chunk, 0, 0)),
        ],
        out_specs=pl.BlockSpec((block, wide), lambda i: (i, 0)),
        compiler_params=params(),
        cost_estimate=cost(2 * total * toks * wide, 2 * (total + toks) * wide),
        name="dispatch",
    )(row, tokens, meta)


def places_kernel(arrived_ref, row_ref, over_ref, top_ref):
    total = arrived_ref.shape[0]
    sources = total // BIN
    spare = ones_where(iota((sources, total), 1) == iota((sources, total), 0) * BIN + (BIN - 1))
    meta = dot(spare, arrived_ref[...]).astype(BF16)
    lane = ones_where(iota((8, 128), 0) == iota((8, 128), 1))
    told = dot_nt(lane, meta)
    n = jnp.where(iota((8, sources), 0) < CHUNK, told, 0.0)
    flagged = jnp.max(jnp.where(iota((8, sources), 0) == CHUNK, told, 0.0))
    each = jnp.sum(n, axis=1, keepdims=True)
    full = (jnp.max(each) > REACH - 1) | (jnp.sum(each) > LIST - 2)
    over = jnp.where((flagged > 0.5) | full, 1.0, 0.0)
    over_ref[...] = jnp.broadcast_to(over, (8, 128))
    top = jnp.broadcast_to(each[0:1] + 1.0, (8, 128))
    high = jnp.floor(top * (1.0 / 128.0))
    lane = iota((8, 128), 1)
    top_ref[...] = jnp.where(lane == 0, high, jnp.where(lane == 1, top - high * 128.0, 0.0))
    base = dot(n.astype(BF16), ones_where(iota((sources, sources), 0) < iota((sources, sources), 1)))
    begin = jnp.zeros((8, sources), F32)
    for j in range(CHUNK):
        ahead = iota((8, sources), 0) > j
        begin = begin + jnp.where(ahead, jnp.broadcast_to(n[j : j + 1], (8, sources)), 0.0)
    shift = base - begin + 128.0
    high = jnp.floor(shift * (1.0 / 128.0))
    low = shift - high * 128.0
    spread = ones_where(iota((sources, total), 1) // BIN == iota((sources, total), 0))
    place = dot(high.astype(BF16), spread) * 128.0 + dot(low.astype(BF16), spread) - 128.0
    begin = dot(begin.astype(BF16), spread)
    end = begin + dot(n.astype(BF16), spread)
    r = (iota((8, total), 1) % BIN).astype(F32)
    place = place + r
    inside = (r >= begin) & (r < end) & (place < REACH - 1) & (r < BIN - 1)
    place = jnp.where(iota((8, total), 0) == 0, place + 1.0, LIST - 2.0 - place)
    index = jnp.where(inside, place + 1.0, 0.0)
    index = jnp.sum(index, axis=0, keepdims=True) - 1.0
    row_ref[...] = jnp.broadcast_to(index, (8, total))


def places(arrived):
    total = arrived.shape[0]
    return pl.pallas_call(
        places_kernel,
        out_shape=(
            jax.ShapeDtypeStruct((8, total), F32),
            jax.ShapeDtypeStruct((8, 128), F32),
            jax.ShapeDtypeStruct((8, 128), F32),
        ),
        grid=(1,),
        in_specs=[pl.BlockSpec((total, 128), lambda i: (0, 0))],
        out_specs=(
            pl.BlockSpec((8, total), lambda i: (0, 0)),
            pl.BlockSpec((8, 128), lambda i: (0, 0)),
            pl.BlockSpec((8, 128), lambda i: (0, 0)),
        ),
        compiler_params=params(),
        cost_estimate=cost(1 << 25, 1 << 19),
        name="places",
    )(arrived)


def regroup_kernel(first, index_ref, rows_ref, top_ref, out_ref):
    count, many = out_ref.shape[0], rows_ref.shape[0]
    begin = first + pl.program_id(0) * count
    here = iota((count, many), 0) + begin
    value = dot(ones_where(here == index_ref[0:1, :].astype(jnp.int32)), rows_ref[...])
    out_ref[...] = value.astype(BF16)
    at = iota((count, 128), 0) + begin
    spare = jnp.where((at == 0) | (at == LIST - 1), top_ref[0:1, :], 0.0)
    out_ref[:, 0:128] = (value[:, 0:128] + spare).astype(BF16)


def regroup(index, rows, top, part):
    many, wide = rows.shape
    first, count = part
    block = 480 if count == LIST else count
    return pl.pallas_call(
        functools.partial(regroup_kernel, first),
        out_shape=jax.ShapeDtypeStruct((count, wide), BF16),
        grid=(count // block,),
        in_specs=[
            pl.BlockSpec((8, many), lambda i: (0, 0)),
            pl.BlockSpec((many, wide), lambda i: (0, 0)),
            pl.BlockSpec((8, 128), lambda i: (0, 0)),
        ],
        out_specs=pl.BlockSpec((block, wide), lambda i: (i, 0)),
        compiler_params=params(),
        cost_estimate=cost(2 * count * many * wide, 2 * (count + many) * wide),
        name="regroup",
    )(index, rows, top)


def weights_kernel(first, in_ref, out_ref, both_ref, held_ref, read_sems, write_sems):
    reads, writes = [], []
    for k, ref in enumerate((in_ref, out_ref)):
        for i in range(CHUNK):
            at = k * CHUNK + i
            reads.append(pltpu.make_async_copy(ref.at[first + i], held_ref.at[at], read_sems.at[at]))
            writes.append(pltpu.make_async_copy(held_ref.at[at], both_ref.at[at], write_sems.at[at]))
    for read in reads:
        read.start()
    for read, write in zip(reads, writes):
        read.wait()
        write.start()
    for write in writes:
        write.wait()


def weights(w_in, w_out, first):
    _, wide, hid = w_in.shape
    shape = (2 * CHUNK, wide, hid)
    return pl.pallas_call(
        functools.partial(weights_kernel, first),
        out_shape=jax.ShapeDtypeStruct(shape, w_in.dtype),
        in_specs=[pl.BlockSpec(memory_space=pl.ANY)] * 2,
        out_specs=pl.BlockSpec(memory_space=pl.ANY),
        scratch_shapes=[
            pltpu.VMEM(shape, w_in.dtype),
            pltpu.SemaphoreType.DMA((2 * CHUNK,)),
            pltpu.SemaphoreType.DMA((2 * CHUNK,)),
        ],
        compiler_params=params(),
        cost_estimate=cost(1, 8 * CHUNK * wide * hid),
        name="weights",
    )(w_in, w_out)


def expert_kernel(parts, *refs):
    n = len(parts)
    rows_refs, weight_refs = refs[:n], refs[n : n + 4]
    part_refs, total_refs = refs[-2 * n : -n], refs[-n:]
    step = pl.program_id(0)
    at = 0 if parts[0][0] == 0 else parts[0][1] - 16
    lane, line = iota((16, 128), 1), iota((16, 128), 0)
    scale = jnp.where(lane == 0, 128.0, jnp.where(lane == 1, 1.0, 0.0))
    scale = jnp.where(line == (0 if at == 0 else 15), scale, 0.0)
    top = jnp.sum(rows_refs[0][at : at + 16, 0:128].astype(F32) * scale).astype(jnp.int32)

    def add(upper, begins):
        in0_ref, out0_ref, in1_ref, out1_ref = weight_refs
        reach = (0, REACH) if upper else (LIST - REACH, LIST)
        for (first, count), rows_ref, total_ref in zip(parts, rows_refs, total_refs):
            low, high = max(reach[0] - first, 0), min(reach[1] - first, count)
            if begins and low > 0:
                total_ref[0:low, :] = jnp.zeros((low, total_ref.shape[1]), F32)
            if begins and high < count:
                total_ref[high:count, :] = jnp.zeros((count - high, total_ref.shape[1]), F32)
            place = iota((high - low, 1), 0) + (first + low)
            mine = place < top if upper else place >= top
            rows = jnp.where(mine, rows_ref[low:high, :], jnp.zeros((), BF16))
            term = None
            for in_ref, out_ref in ((in0_ref, out0_ref), (in1_ref, out1_ref)):
                hidden = jnp.maximum(dot(rows, in_ref[0]), 0.0).astype(BF16)
                part = dot(hidden, out_ref[0])
                term = part if term is None else term + part
            total_ref[low:high, :] = term if begins else total_ref[low:high, :] + term

    for k in range(CHUNK):

        @pl.when(step == k)
        def _(k=k):
            add(k == 0, k == 0)
            if k == CHUNK - 1:
                for part_ref, total_ref in zip(part_refs, total_refs):
                    part_ref[...] = total_ref[...].astype(part_ref.dtype)


def expert(rows, parts, w_in, w_out, first, other, dtype, later_than=()):
    wide, hid = w_in.shape[1], w_in.shape[2]
    total = sum(count for _, count in parts)
    wholes = [pl.BlockSpec((count, wide), lambda i: (0, 0)) for _, count in parts]
    made = pl.pallas_call(
        functools.partial(expert_kernel, parts),
        out_shape=[jax.ShapeDtypeStruct((count, wide), dtype) for _, count in parts],
        grid=(CHUNK,),
        in_specs=wholes
        + [
            pl.BlockSpec((1, wide, hid), lambda i: (first + i, 0, 0)),
            pl.BlockSpec((1, hid, wide), lambda i: (first + i, 0, 0)),
            pl.BlockSpec((1, wide, hid), lambda i: (i, 0, 0)),
            pl.BlockSpec((1, hid, wide), lambda i: (CHUNK + i, 0, 0)),
        ]
        + [pl.BlockSpec(memory_space=pl.ANY)] * len(later_than),
        out_specs=wholes,
        scratch_shapes=[pltpu.VMEM((count, wide), F32) for _, count in parts],
        compiler_params=pltpu.CompilerParams(vmem_limit_bytes=32 * 1024 * 1024),
        cost_estimate=cost(8 * total * wide * hid, 8 * CHUNK * wide * hid + 6 * total * wide),
        name="expert",
    )(*rows, w_in, w_out, other, other, *later_than)
    return list(made)


def back_kernel(parts, index_ref, over_ref, *refs):
    n, out_ref = len(parts), refs[-1]
    rows = out_ref.shape[0]
    col = turned(index_ref[...])[:, 0:1].astype(jnp.int32)
    result = None
    for i, (first, count) in enumerate(parts):
        value = (refs[i][...] + refs[n + i][...].astype(F32)).astype(BF16)
        part = dot(ones_where(col - first == iota((rows, count), 1)), value)
        result = part if result is None else result + part
    out_ref[...] = result.astype(BF16)
    at = iota((rows, 128), 0) + pl.program_id(0) * rows
    flag = jnp.where(at % BIN == BIN - 1, over_ref[0:1, :], 0.0)
    out_ref[:, 0:128] = (result[:, 0:128] + flag).astype(BF16)


def back(index, own, sent, over, parts):
    total, wide = index.shape[1], own[0].shape[1]
    block = total // 2
    wholes = [pl.BlockSpec((count, wide), lambda i: (0, 0)) for _, count in parts]
    return pl.pallas_call(
        functools.partial(back_kernel, parts),
        out_shape=jax.ShapeDtypeStruct((total, wide), BF16),
        grid=(total // block,),
        in_specs=[
            pl.BlockSpec((8, block), lambda i: (0, i)),
            pl.BlockSpec((8, 128), lambda i: (0, 0)),
        ]
        + wholes * 2,
        out_specs=pl.BlockSpec((block, wide), lambda i: (i, 0)),
        compiler_params=params(),
        cost_estimate=cost(2 * total * LIST * wide, 2 * total * wide + 6 * LIST * wide),
        name="back",
    )(index, over, *own, *sent)


def combine_kernel(chunk, last, row_ref, returned_ref, *refs):
    out_ref = refs[-1] if last else refs[-2]
    rows, many = out_ref.shape[0], returned_ref.shape[0]
    cols = turned(row_ref[...])
    col = cols[:, 0:1].astype(jnp.int32) - chunk * many
    total = dot(ones_where(col == iota((rows, many), 1)), returned_ref[...])
    if chunk > 0:
        total = total + refs[0][...].astype(F32)
    if last:
        out_ref[...] = (total * cols[:, 1:2]).astype(BF16)
        return
    out_ref[...] = total.astype(BF16)
    spare = iota((many, 128), 0) % BIN == BIN - 1
    over = jnp.max(jnp.where(spare, returned_ref[:, 0:128].astype(F32), 0.0))
    refs[-1][...] = jnp.broadcast_to(over, (8, 128))


def combine(row, returned, chunk, last, so_far):
    toks, (many, wide) = row.shape[1], returned.shape
    block = toks // 2
    extra = [] if so_far is None else [so_far]
    tokens_out = (jax.ShapeDtypeStruct((toks, wide), BF16), pl.BlockSpec((block, wide), lambda i: (i, 0)))
    flag_out = (jax.ShapeDtypeStruct((8, 128), F32), pl.BlockSpec((8, 128), lambda i: (0, 0)))
    shapes, specs = zip(*([tokens_out] if last else [tokens_out, flag_out]))
    return pl.pallas_call(
        functools.partial(combine_kernel, chunk, last),
        out_shape=shapes,
        grid=(toks // block,),
        in_specs=[
            pl.BlockSpec((8, block), lambda i: (0, i)),
            pl.BlockSpec((many, wide), lambda i: (0, 0)),
        ]
        + [pl.BlockSpec((block, wide), lambda i: (i, 0))] * len(extra),
        out_specs=specs,
        compiler_params=params(),
        cost_estimate=cost(2 * toks * many * wide, 2 * (many + 2 * toks) * wide),
        name="combine",
    )(row, returned, *extra)


def assign(first, backup, capacity, count, slot):
    columns = jnp.arange(count, dtype=jnp.int32)
    where = jnp.arange(first.shape[0], dtype=jnp.int32)
    earlier = ones_where(where[None, :] < where[:, None])
    onehot = (first[:, None] == columns[None, :]).astype(F32)
    rank = jnp.sum(dot(earlier, onehot.astype(BF16)) * onehot, axis=1)
    limit = jnp.sum(onehot * capacity[None, :].astype(F32), axis=1)
    kept = rank < limit
    spill = jnp.where((backup[:, None] == columns[None, :]) & ~kept[:, None], 1.0, 0.0)
    spill_rank = jnp.sum(dot(earlier, spill.astype(BF16)) * spill, axis=1)
    final = jnp.where(kept, first, backup)
    slots = jnp.where(kept, rank, slot + spill_rank).astype(jnp.int32)
    return slots, final


def general(tokens, gate, first, backup, capacity, w_in, w_out):
    held = w_in.shape[0]
    owners = lax.axis_size(EXPERT)
    helpers = lax.axis_size("helper")
    experts = held * owners
    slot = max(6, 3 * tokens.shape[0] // (2 * experts))
    slots, final = assign(first, backup, capacity, experts, slot)
    wide = tokens.shape[1]
    buffer = jnp.zeros((experts, 2 * slot, wide), BF16).at[final, slots].set(tokens)
    buffer = buffer.reshape(owners, held * 2 * slot, wide)
    arrived = lax.all_to_all(buffer, EXPERT, 0, 0, tiled=True)
    arrived = arrived.reshape(owners, held, 2 * slot, wide)
    rows = [arrived[:, e].reshape(owners * 2 * slot, wide) for e in range(held)]
    totals = [jnp.zeros(r.shape, F32) for r in rows]
    for k in range(helpers):
        turn = [(i, (i + k) % helpers) for i in range(helpers)]
        some_in = lax.ppermute(w_in, "helper", turn) if k else w_in
        some_out = lax.ppermute(w_out, "helper", turn) if k else w_out
        for e in range(held):
            hidden = jnp.maximum(dot(rows[e], some_in[e]), 0.0).astype(BF16)
            totals[e] = totals[e] + dot(hidden, some_out[e]).astype(BF16).astype(F32)
    outputs = [t.astype(BF16).reshape(owners, 2 * slot, wide) for t in totals]
    result = jnp.stack(outputs, axis=1).reshape(owners, held * 2 * slot, wide)
    returned = lax.all_to_all(result, EXPERT, 0, 0, tiled=True)
    picked = returned.reshape(experts, 2 * slot, wide)[final, slots]
    return (gate[:, None] * picked.astype(F32)).astype(BF16)


def after(*values):
    return lax.optimization_barrier(values)


def on_device(tokens, gate, expert_ids, backup_ids, capacity, w_in, w_out):
    held = w_in.shape[0]
    owners = lax.axis_size(EXPERT)
    helpers = lax.axis_size("helper")
    toks, wide = tokens.shape
    chunks = range(held // CHUNK)
    w_parts = [weights(w_in, w_out, c * CHUNK) for c in chunks]
    others = [lax.ppermute(w, CORE_X, NEAR) for w in w_parts]
    row, meta = route(
        expert_ids.reshape(1, toks),
        backup_ids.reshape(1, toks),
        capacity.reshape(1, -1),
        gate.reshape(1, toks),
        held,
    )

    def exchange(rows):
        rows = lax.all_to_all(rows.reshape(owners, BIN, wide), EXPERT, 0, 0, tiled=True)
        return rows.reshape(owners * BIN, wide)

    arrived = [exchange(dispatch(row, tokens, meta, c, held)) for c in chunks]
    at_row, overs, tops = zip(*[places(a) for a in arrived])
    rows = [[regroup(at_row[c], arrived[c], tops[c], p) for p in PARTS[c]] for c in chunks]
    theirs = [[lax.ppermute(r, CORE_X, FAR) for r in rows[c]] for c in chunks]
    over = functools.reduce(jnp.maximum, overs)
    own, sent = [], []
    for c in chunks:
        k = c * CHUNK
        args = (w_in, w_out, k, others[c])
        made = [expert([t], [p], *args, BF16)[0] for t, p in zip(theirs[c], PARTS[c])]
        sent.append([lax.ppermute(m, CORE_X, FAR) for m in made])
        ahead = rows[c + 1] if c < chunks[-1] else []
        own.append(expert(rows[c], PARTS[c], *args, F32, ahead))
    mixed, flags = None, []
    for c in chunks:
        returned = exchange(back(at_row[c], own[c], sent[c], over, PARTS[c]))
        mixed, *flag = combine(row, returned, c, c == chunks[-1], mixed)
        flags += flag
    around = [[(i, (i + k) % helpers) for i in range(helpers)] for k in range(1, helpers)]
    over = functools.reduce(jnp.maximum, [flags[0]] + [lax.ppermute(flags[0], "helper", a) for a in around])
    return lax.cond(
        over[0, 0] > 0.5,
        lambda ops: general(*ops[1:]),
        lambda ops: ops[0],
        (mixed, tokens, gate, expert_ids[:, 0], backup_ids[:, 0], capacity, w_in, w_out),
    )


def solution(mesh):
    torus = Mesh(
        mesh.devices.reshape(4, 4, 2, mesh.shape["helper"]),
        ("expert_0", "expert_1", "expert_2", "helper"),
    )
    in_specs = (
        P(EXPERT_HELPER, None),
        P(EXPERT_HELPER),
        P(EXPERT_HELPER, None),
        P(EXPERT_HELPER, None),
        P(),
        P(EXPERT, None, "helper"),
        P(EXPERT, "helper", None),
    )
    out_specs = P(EXPERT_HELPER, None)
    return jax.shard_map(
        on_device, mesh=torus, in_specs=in_specs, out_specs=out_specs, check_vma=False
    )
```
